32 devices in a mesh: groups: 2 (over y), patch: 8 (over z, x), req: 2 (over core).
Axes of the slice: x: 2, y: 2, z: 4, core: 2. Of those that a mesh axis runs over, the one named last changes fastest.
Arguments:
- hidden: float32 [16, 8, 64, 1280], P(('groups', 'req'), 'patch'), parts along dimension 0
- skip: float32 [16, 8, 64, 1280], P(('groups', 'req'), 'patch'), parts along dimension 0, may hold values from -6 to 6
- timestep_embedding_table: float32 [50, 1280], replicated, may hold values from -5 to 5
- timesteps: int32 [16], P(('groups', 'req')), parts along dimension 0, may hold values from 0 to 49, as said below
- group_norm_gain: float32 [1280], replicated, may hold values from 0.1 to 1.9
- group_norm_bias: float32 [1280], replicated, may hold values from -3 to 3
- kernel_weight: bfloat16 [9, 1280, 1280], P(None, 'patch', 'req'), may hold values from -0.0546875 to 0.0546875
- adapter_down_weight: bfloat16 [32, 64, 11520], P(('groups', 'patch')), parts along dimension 0, may hold values from -0.0546875 to 0.0546875
- adapter_up_weight: bfloat16 [32, 64, 1280], P(('groups', 'patch')), parts along dimension 0, may hold values from -0.75 to 0.75
- request_adapter: int32 [16], P(('groups', 'req')), parts along dimension 0, may hold values from 0 to 15
- adapter_row_table: int32 [32], P('groups'), parts along dimension 0, may hold values from 0 to 15, each once
Outputs:
- block_out: float32 [16, 8, 64, 1280], P(('groups', 'req'), 'patch'), parts along dimension 0
The draws below stay inside these ranges and needn't reach their ends.
There are 2 independent parts, one for each index of `groups`. The reference program is written for one: setup_inputs(seed, part) draws one part's arguments, and reference() takes and returns one part's arrays. A program takes and returns all parts, laid end to end along the dimension named above; an argument that names none is the same for every part. Nothing has to cross between parts.
Inputs may be any that keep to these rules, and one draw needn't show every extreme that they name: adapter_row_table[a] is the store row of adapter a; every row is used once. Requests 0 and 1 have different timesteps.
All inputs are finite; a program needn't handle non-finite values.
Results may differ from the reference program's by a relative error of at most 0.0026.
Values may be sent and summed in bfloat16 or wider, within the bound.
A program may use at most 128 MiB of HBM per device.

```python
import math
import jax
import jax.numpy as jnp
import numpy as np
from jax import lax

CHANNEL_COUNT = 1280
GROUPS = 32
ADAPTER_RANK = 64
W = 64
STEPS = 50
H = 8
REQUESTS = 8
ADAPTER_COUNT = 16


def draw_hidden(key, part):
    key_base = jax.random.fold_in(key, 11)
    key_chan = jax.random.fold_in(key, 12)
    base = jax.random.normal(key_base, (REQUESTS, H, W, CHANNEL_COUNT), jnp.float32)
    row_scale = 3.0 ** (jnp.arange(H, dtype=jnp.float32) / max(H - 1, 1))
    chan_scale = jnp.exp(jax.random.uniform(key_chan, (CHANNEL_COUNT,), jnp.float32, -0.7, 0.7))
    return base * row_scale[None, :, None, None] * chan_scale[None, None, None, :]


def draw_timesteps(key, part):
    key_all = jax.random.fold_in(key, 21)
    key_off = jax.random.fold_in(key, 22)
    values = jax.random.randint(key_all, (REQUESTS,), 0, STEPS, dtype=jnp.int32)
    offset = jax.random.randint(key_off, (), 0, STEPS - 1, dtype=jnp.int32)
    second = (values[0] + 1 + offset) % STEPS
    return values.at[1].set(second.astype(jnp.int32))


def plant(entries, rng, low, top_value):
    longest = entries.shape.index(max(entries.shape))
    spots = []
    for shift in (0, 1):
        where = [jax.random.randint(jax.random.fold_in(rng, axis), (), 0, length) for axis, length in enumerate(entries.shape)]
        where[longest] = (where[longest] + shift) % entries.shape[longest]
        spots.append(tuple(where))
    return entries.at[spots[0]].set(low).at[spots[1]].set(top_value)


def shard_levels(rng, dims, shards, least, top_value):
    factor_of, own = 1.0, jax.random.fold_in(rng, 6)
    for axis_at, shards_of in shards:
        steps = jnp.exp(jax.random.uniform(jax.random.fold_in(own, axis_at), (shards_of,), jnp.float32, least / len(shards), top_value / len(shards)))
        factor_of = factor_of * jnp.repeat(steps, dims[axis_at] // shards_of).reshape([-1 if axis == axis_at else 1 for axis in range(len(dims))])
    return factor_of


def rank_bounds(count, lean):
    portions = [(1 << 20) // math.isqrt(grade ** lean) + 1 for grade in range(1, count + 1)]
    scale = 1 + sum(portions) // (1 << 30)
    return np.cumsum(np.array([max(1, weight // scale) for weight in portions]))


def ranked_ids(key, shape, amount, slope):
    grid = rank_bounds(amount, slope)
    pick = jax.random.randint(jax.random.fold_in(key, 1), shape, 0, int(grid[amount - 1]))
    standing = jnp.searchsorted(jnp.asarray(grid, jnp.int32), pick, side="right")
    return jax.random.permutation(jax.random.fold_in(key, 2), amount)[standing].astype(jnp.int32)


def gaussian(stream_key, shape, scale, limit, shards=(), held_as=jnp.bfloat16):
    loudness = shard_levels(stream_key, shape, shards, -0.22, 0.18) if shards else 1.0
    result = jax.random.normal(stream_key, shape, jnp.float32) * scale * loudness
    return jnp.minimum(jnp.maximum(result, -limit), limit).astype(held_as)


def setup_inputs(seed: int = 0, part: int = 0) -> dict:
    keys = jax.random.split(jax.random.key(seed), 12)
    part_splits = jax.random.split(jax.random.fold_in(keys[11], part), 12)
    return {
        "hidden": draw_hidden(jax.random.fold_in(jax.random.fold_in(keys[11], part), 71), part),
        "skip": gaussian(part_splits[1], (REQUESTS, H, W, CHANNEL_COUNT), 1.0, 6.0, ((0, 2), (1, 8)), jnp.float32),
        "timestep_embedding_table": gaussian(keys[2], (STEPS, CHANNEL_COUNT), 1.0, 5.0, (), jnp.float32),
        "timesteps": draw_timesteps(jax.random.fold_in(jax.random.fold_in(keys[11], part), 71), part),
        "group_norm_gain": jnp.clip(1.0 + 0.18 * jax.random.normal(keys[4], (CHANNEL_COUNT,), jnp.float32), 0.1, 1.9),
        "group_norm_bias": gaussian(keys[5], (CHANNEL_COUNT,), 0.5, 3.0, (), jnp.float32),
        "kernel_weight": gaussian(keys[6], (9, CHANNEL_COUNT, CHANNEL_COUNT), (9 * CHANNEL_COUNT) ** -0.5, 0.0546875, ((1, 8), (2, 2))),
        "adapter_down_weight": gaussian(part_splits[7], (ADAPTER_COUNT, ADAPTER_RANK, 9 * CHANNEL_COUNT), (9 * CHANNEL_COUNT) ** -0.5, 0.0546875, ((0, 8),)),
        "adapter_up_weight": gaussian(part_splits[8], (ADAPTER_COUNT, ADAPTER_RANK, CHANNEL_COUNT), ADAPTER_RANK ** -0.5, 0.75, ((0, 8),)),
        "request_adapter": plant(ranked_ids(part_splits[9], (REQUESTS,), ADAPTER_COUNT, 2), jax.random.fold_in(part_splits[9], 3), 0, ADAPTER_COUNT - 1).astype(jnp.int32),
        "adapter_row_table": jax.random.permutation(part_splits[10], ADAPTER_COUNT).astype(jnp.int32),
    }


def make_taps(act):
    height, width, chans = act.shape
    padded = jnp.pad(act, ((1, 1), (1, 1), (0, 0)))
    pieces = [padded[dy:dy + height, dx:dx + width, :] for dy in range(3) for dx in range(3)]
    return jnp.stack(pieces, axis=2).reshape(height * width, 9 * chans)

def reference(hidden, skip, timestep_embedding_table, timesteps, group_norm_gain, group_norm_bias, kernel_weight, adapter_down_weight, adapter_up_weight, request_adapter, adapter_row_table):
    temb = jnp.take(timestep_embedding_table, timesteps, axis=0)
    shifted = hidden + temb[:, None, None, :]
    request_total, height, width, chans = shifted.shape
    grouped = shifted.reshape(request_total, height, width, GROUPS, chans // GROUPS)
    mean = lax.optimization_barrier(jnp.mean(grouped, axis=(1, 2, 4), keepdims=True))
    centered = grouped - mean
    var = lax.optimization_barrier(jnp.mean(centered * centered, axis=(1, 2, 4), keepdims=True))
    normed = (centered * lax.rsqrt(var + 1e-05)).reshape(request_total, height, width, chans)
    act = jax.nn.silu(normed * group_norm_gain + group_norm_bias).astype(jnp.bfloat16)
    weight = kernel_weight.reshape(9 * chans, chans)
    store_rows = jnp.take(adapter_row_table, request_adapter, axis=0).astype(jnp.int32)

    def single(items):
        one_act, resident_row = items
        taps = make_taps(one_act)
        base = jnp.dot(taps, weight, preferred_element_type=jnp.float32)
        down_factor = lax.dynamic_index_in_dim(adapter_down_weight, resident_row, 0, keepdims=False)
        upper_limit = lax.dynamic_index_in_dim(adapter_up_weight, resident_row, 0, keepdims=False)
        low = lax.dot_general(taps, down_factor, (((1,), (1,)), ((), ())), preferred_element_type=jnp.float32).astype(jnp.bfloat16)
        delta = jnp.dot(low, upper_limit, preferred_element_type=jnp.float32)
        return (base + delta).reshape(height, width, chans)
    conv = lax.map(single, (act, store_rows))
    return skip + conv
```

```python
import functools

import jax
import jax.numpy as jnp
from jax import lax
from jax.experimental import pallas as pl
from jax.experimental.pallas import tpu as pltpu
from jax.sharding import PartitionSpec as P

GROUPS = 32
LANES = 128
WIN = 256
MESH = pl.DeviceIdType.MESH
BF = jnp.bfloat16
F32 = jnp.float32


def hi_dot(a, b, dims):
    return lax.dot_general(
        a, b, (dims, ((), ())), precision=lax.Precision.HIGHEST, preferred_element_type=F32
    )


def block_kernel(
    n, own, reqs, width, chans,
    sel, hid, temb, gain, bias, w_hbm, d_hbm,
    base_out, low_out,
    act, acts_in, taps, wpad, dall, stat_out, stat_in,
    xsend, xrecv, keep, zsend, zrecv, lsend, lrecv,
    st_s, st_r, ac_s, ac_r, ac_l, d_s, d_r, d_l, w_s, w_r, w_l, dp_s, dp_r,
    x_s, x_r, z_s, z_r, l_s, l_r,
):
    me = lax.axis_index("patch")
    core = lax.axis_index("req")
    mate = 1 - core
    zs = n // 2
    z, x = me // 2, me % 2
    half = chans // 2
    rank = dall.shape[1]
    hrank = rank // 2
    per = n and d_hbm.shape[0]

    def window(j):
        return pl.multiple_of((j * own) // LANES * LANES, LANES)

    wpad[...] = jnp.zeros_like(wpad)

    barrier = pltpu.get_barrier_semaphore()
    for k in range(1, n):
        pl.semaphore_signal(barrier, inc=1, device_id={"patch": (me + k) % n}, device_id_type=MESH)
    pl.semaphore_signal(barrier, inc=1, device_id={"req": mate}, device_id_type=MESH)
    pl.semaphore_wait(barrier, n)

    inner = pl.multiple_of((me * own) % LANES, 32)

    def w_dst(t, c):
        return wpad.at[
            t // 3,
            pl.ds(pl.multiple_of((t % 3) * WIN + inner, 32), own),
            pl.ds(pl.multiple_of(c * half, LANES), half),
        ]

    def w_remote(t, c):
        return pltpu.make_async_remote_copy(
            src_ref=w_hbm.at[t], dst_ref=w_dst(t, c), send_sem=w_s.at[t], recv_sem=w_r.at[t],
            device_id={"req": mate}, device_id_type=MESH,
        )

    def w_local(t):
        return pltpu.make_async_copy(w_hbm.at[t], w_dst(t, core), w_l.at[t])

    for t in range(9):
        w_local(t).start()
        w_remote(t, core).start()

    c_of = lax.broadcasted_iota(jnp.int32, (chans, LANES), 0)
    g_of = lax.broadcasted_iota(jnp.int32, (chans, LANES), 1)
    size = chans // GROUPS
    member = jnp.where((c_of >= g_of * size) & (c_of < (g_of + 1) * size), 1.0, 0.0).astype(F32)
    count = width * size
    sums = [
        jnp.sum(hid[r * width : (r + 1) * width, :] + temb[r : r + 1, :], axis=0, keepdims=True)
        for r in range(reqs)
    ]
    pad = [jnp.zeros((8 - reqs, chans), F32)] if reqs < 8 else []
    mean = hi_dot(jnp.concatenate(sums + pad, axis=0), member, ((1,), (0,))) / count
    wide = hi_dot(mean, member, ((1,), (1,)))
    squares = []
    for r in range(reqs):
        c = hid[r * width : (r + 1) * width, :] + temb[r : r + 1, :] - wide[r : r + 1, :]
        squares.append(jnp.sum(c * c, axis=0, keepdims=True))
    second = hi_dot(jnp.concatenate(squares + pad, axis=0), member, ((1,), (0,)))
    stat_out[0] = mean
    stat_out[1] = second

    def st_copy(peer, src):
        return pltpu.make_async_remote_copy(
            src_ref=stat_out, dst_ref=stat_in.at[src], send_sem=st_s.at[peer], recv_sem=st_r.at[src],
            device_id={"patch": peer}, device_id_type=MESH,
        )

    for k in range(1, n):
        st_copy((me + k) % n, me).start()
    stat_in[me] = stat_out[...]
    for k in range(1, n):
        st_copy((me + k) % n, (me + k) % n).wait_recv()
    means = stat_in[:, 0]
    total_mean = jnp.sum(means, axis=0) / n
    spread = means - total_mean[None]
    var = (jnp.sum(stat_in[:, 1], axis=0) + count * jnp.sum(spread * spread, axis=0)) / (count * n)
    mean_w = hi_dot(total_mean, member, ((1,), (1,)))
    inv_w = hi_dot(lax.rsqrt(var + 1e-05), member, ((1,), (1,)))
    for r in range(reqs):
        rows = slice(r * width, (r + 1) * width)
        v = (hid[rows, :] + temb[r : r + 1, :] - mean_w[r : r + 1, :]) * inv_w[r : r + 1, :]
        v = v * gain[...] + bias[...]
        act[rows, :] = (v / (1.0 + jnp.exp(-v))).astype(BF)

    def ac_copy(peer, src):
        return pltpu.make_async_remote_copy(
            src_ref=act.at[:, pl.ds(window(peer), WIN)], dst_ref=acts_in.at[src],
            send_sem=ac_s.at[peer], recv_sem=ac_r.at[src],
            device_id={"patch": peer}, device_id_type=MESH,
        )

    ac_own = pltpu.make_async_copy(act.at[:, pl.ds(window(me), WIN)], acts_in.at[me], ac_l)
    for k in range(1, n):
        ac_copy((me + k) % n, me).start()
    ac_own.start()

    rank_at = pl.multiple_of(core * hrank, hrank)

    def d_src(t, peer):
        return d_hbm.at[:, pl.ds(rank_at, hrank), pl.ds(pl.multiple_of(t * chans + window(peer), LANES), WIN)]

    def d_dst(t, src):
        return dall.at[pl.ds(src * per, per), pl.ds(rank_at, hrank), pl.ds(pl.multiple_of(t * WIN, WIN), WIN)]

    def d_copy(t, peer, src):
        return pltpu.make_async_remote_copy(
            src_ref=d_src(t, peer), dst_ref=d_dst(t, src),
            send_sem=d_s.at[peer, t], recv_sem=d_r.at[src, t],
            device_id={"patch": peer}, device_id_type=MESH,
        )

    def d_own(t):
        return pltpu.make_async_copy(d_src(t, me), d_dst(t, me), d_l.at[t])

    @pl.loop(0, 9)
    def _(t):
        d_own(t).start()

        @pl.loop(1, n)
        def _(k):
            d_copy(t, (me + k) % n, me).start()

    taps[0] = jnp.zeros(taps.shape[1:], BF)
    taps[n + 1] = jnp.zeros(taps.shape[1:], BF)
    cells = reqs * width
    px = lax.broadcasted_iota(jnp.int32, (cells, WIN), 0) % width
    ch = lax.broadcasted_iota(jnp.int32, (cells, WIN), 1)
    mine = (ch >= inner) & (ch < inner + own)

    def lay(y):
        v = jnp.where(mine, acts_in[y].astype(F32), 0.0)
        taps[y + 1, :, 0:WIN] = jnp.where(px == 0, 0.0, pltpu.roll(v, 1, 0)).astype(BF)
        taps[y + 1, :, WIN : 2 * WIN] = v.astype(BF)
        taps[y + 1, :, 2 * WIN :] = jnp.where(px == width - 1, 0.0, pltpu.roll(v, cells - 1, 0)).astype(BF)

    ac_own.wait()
    lay(me)

    @pl.loop(1, n)
    def _(k):
        y = (me + k) % n
        ac_copy(y, y).wait_recv()
        lay(y)

    for t in range(9):
        w_local(t).wait()
        w_remote(t, mate).wait_recv()

    def conv(y, put):
        @pl.loop(0, chans // WIN)
        def _(m):
            cols = pl.ds(pl.multiple_of(m * WIN, WIN), WIN)
            s = jnp.dot(taps[y], wpad[0, :, cols], preferred_element_type=F32)
            s += jnp.dot(taps[y + 1], wpad[1, :, cols], preferred_element_type=F32)
            s += jnp.dot(taps[y + 2], wpad[2, :, cols], preferred_element_type=F32)
            put(cols, s)

    def x_copy(i):
        return pltpu.make_async_remote_copy(
            src_ref=xsend.at[i], dst_ref=xrecv.at[i], send_sem=x_s.at[i], recv_sem=x_r.at[i],
            device_id={"patch": me + 1 - 2 * x}, device_id_type=MESH,
        )

    def z_copy(i, zt, src):
        return pltpu.make_async_remote_copy(
            src_ref=zsend.at[i], dst_ref=zrecv.at[src], send_sem=z_s.at[i], recv_sem=z_r.at[src],
            device_id={"patch": zt * 2 + x}, device_id_type=MESH,
        )

    def forward(i):
        x_copy(i).wait_recv()
        zsend[i] = (keep[...] + xrecv[i].astype(F32)).astype(BF)
        z_copy(i, (z + 1 + i) % zs, z).start()

    @pl.loop(0, zs)
    def _(i):
        zt = (z + 1 + i) % zs

        def put_x(cols, s):
            xsend[i, :, cols] = s.astype(BF)

        conv(zt * 2 + 1 - x, put_x)
        x_copy(i).start()

        def put_keep(cols, s):
            keep[:, cols] = s

        conv(zt * 2 + x, put_keep)

        @pl.when(i < zs - 1)
        def _():
            forward(i)

    x_copy(zs - 1).wait_recv()
    base_out[...] = keep[...] + xrecv[zs - 1].astype(F32)

    @pl.loop(0, 9)
    def _(t):
        d_own(t).wait()

        @pl.loop(1, n)
        def _(k):
            d_copy(t, (me + k) % n, (me + k) % n).wait_recv()

    def dp_copy(at):
        part = dall.at[:, pl.ds(pl.multiple_of(at * hrank, hrank), hrank), :]
        return pltpu.make_async_remote_copy(
            src_ref=part, dst_ref=part, send_sem=dp_s, recv_sem=dp_r,
            device_id={"req": mate}, device_id_type=MESH,
        )

    dp_copy(core).start()
    dp_copy(mate).wait_recv()
    for r in range(reqs):
        factor = dall[sel[r]]
        low = jnp.zeros((n * width, rank), F32)
        for dy in range(3):
            lhs = taps[dy : dy + n, r * width : (r + 1) * width, :].reshape(n * width, 3 * WIN)
            low += lax.dot_general(
                lhs, factor[:, dy * 3 * WIN : (dy + 1) * 3 * WIN], (((1,), (1,)), ((), ())),
                preferred_element_type=F32,
            )
        high = low.astype(BF).astype(F32)
        both = jnp.concatenate([high, low - high], axis=1).astype(BF)
        lsend[:, r * width : (r + 1) * width, :] = both.reshape(n, width, 2 * rank)

    def l_copy(peer, src):
        return pltpu.make_async_remote_copy(
            src_ref=lsend.at[peer], dst_ref=lrecv.at[src], send_sem=l_s.at[peer], recv_sem=l_r.at[src],
            device_id={"patch": peer}, device_id_type=MESH,
        )

    for k in range(1, n):
        l_copy((me + k) % n, me).start()

    @pl.loop(1, zs)
    def _(k):
        src = (z + k) % zs
        z_copy(0, src, src).wait_recv()
        base_out[...] += zrecv[src].astype(F32)

    both = lsend[me].astype(F32)
    for k in range(1, n):
        src = (me + k) % n
        l_copy(src, src).wait_recv()
        both += lrecv[src].astype(F32)
    low_out[...] = (both[:, :rank] + both[:, rank:]).astype(BF)

    dp_copy(core).wait_send()
    for t in range(9):
        w_remote(t, core).wait_send()
    for k in range(1, n):
        st_copy((me + k) % n, me).wait_send()
        ac_copy((me + k) % n, me).wait_send()
        l_copy((me + k) % n, me).wait_send()

    @pl.loop(0, 9)
    def _(t):
        @pl.loop(1, n)
        def _(k):
            d_copy(t, (me + k) % n, me).wait_send()

    @pl.loop(0, zs)
    def _(i):
        x_copy(i).wait_send()

    @pl.loop(0, zs - 1)
    def _(i):
        z_copy(i, (z + 1 + i) % zs, z).wait_send()


def conv_and_low(n, sel, hid, temb, gain, bias, weight, down):
    cells, chans = hid.shape
    reqs = sel.shape[0]
    width = cells // reqs
    own = weight.shape[1]
    per, rank, _ = down.shape
    zs = n // 2
    dma = pltpu.SemaphoreType.DMA
    vmem = pl.BlockSpec(memory_space=pltpu.VMEM)
    hbm = pl.BlockSpec(memory_space=pl.ANY)
    return pl.pallas_call(
        functools.partial(block_kernel, n, own, reqs, width, chans),
        out_shape=(
            jax.ShapeDtypeStruct((cells, chans), F32),
            jax.ShapeDtypeStruct((cells, rank), BF),
        ),
        in_specs=[pl.BlockSpec(memory_space=pltpu.SMEM), vmem, vmem, vmem, vmem, hbm, hbm],
        out_specs=(vmem, vmem),
        scratch_shapes=[
            pltpu.VMEM((cells, chans), BF),
            pltpu.VMEM((n, cells, WIN), BF),
            pltpu.VMEM((n + 2, cells, 3 * WIN), BF),
            pltpu.VMEM((3, 3 * WIN, chans), BF),
            pltpu.VMEM((n * per, rank, 9 * WIN), BF),
            pltpu.VMEM((2, 8, LANES), F32),
            pltpu.VMEM((n, 2, 8, LANES), F32),
            pltpu.VMEM((zs, cells, chans), BF),
            pltpu.VMEM((zs, cells, chans), BF),
            pltpu.VMEM((cells, chans), F32),
            pltpu.VMEM((zs - 1, cells, chans), BF),
            pltpu.VMEM((zs, cells, chans), BF),
            pltpu.VMEM((n, cells, 2 * rank), BF),
            pltpu.VMEM((n, cells, 2 * rank), BF),
            dma((n,)), dma((n,)),
            dma((n,)), dma((n,)), dma,
            dma((n, 9)), dma((n, 9)), dma((9,)),
            dma((9,)), dma((9,)), dma((9,)),
            dma, dma,
            dma((zs,)), dma((zs,)),
            dma((zs - 1,)), dma((zs,)),
            dma((n,)), dma((n,)),
        ],
        compiler_params=pltpu.CompilerParams(
            collective_id=0, has_side_effects=True, vmem_limit_bytes=56 * 2**20
        ),
        cost_estimate=pl.CostEstimate(
            flops=2 * n * cells * 9 * WIN * chans, bytes_accessed=10**8, transcendentals=0
        ),
    )(sel, hid, temb, gain, bias, weight, down)


def split_contraction(
    hidden, skip, timestep_embedding_table, timesteps, group_norm_gain, group_norm_bias,
    kernel_weight, adapter_down_weight, adapter_up_weight, request_adapter, adapter_row_table,
):
    n = lax.axis_size("patch")
    reqs, rows, width, chans = hidden.shape
    per = adapter_up_weight.shape[0]
    sel = adapter_row_table[request_adapter]
    temb = timestep_embedding_table[timesteps]
    spot = jnp.clip(sel - lax.axis_index("patch") * per, 0, per - 1)
    here = (sel // per == lax.axis_index("patch"))[:, None, None]
    up = lax.psum(jnp.where(here, adapter_up_weight[spot], jnp.zeros((), BF)), "patch")
    base, low = conv_and_low(
        n, sel, hidden.reshape(reqs * width, chans), temb, group_norm_gain[None],
        group_norm_bias[None], kernel_weight, adapter_down_weight,
    )
    delta = jnp.einsum("rpk,rkc->rpc", low.reshape(reqs, width, -1), up, preferred_element_type=F32)
    return skip + (base.reshape(reqs, width, chans) + delta).reshape(hidden.shape)


def fits(n, hidden, kernel_weight, down):
    own = kernel_weight.shape[1]
    ends = all(j * own // LANES * LANES + WIN <= hidden.shape[3] and j * own % LANES + own <= WIN for j in range(n))
    return (
        n % 2 == 0 and n <= 8 and hidden.shape[1] == 1 and hidden.shape[0] <= 8
        and own % 32 == 0 and ends and down.shape[1] == 64
    )


def broadcast(block, axis, owner):
    block = jnp.where(lax.axis_index(axis) == owner, block, jnp.zeros_like(block))
    return lax.psum(block, axis)


def padded(cells, sides, width):
    for axis, dim in sides:
        count = lax.axis_size(axis)
        ends = count - 1
        head = lax.slice_in_dim(cells, 0, width, axis=dim)
        tail = lax.slice_in_dim(cells, cells.shape[dim] - width, cells.shape[dim], axis=dim)
        cells = jnp.concatenate(
            [
                lax.ppermute(tail, axis, [(i, (i + 1) % count) for i in range(ends)]),
                cells,
                lax.ppermute(head, axis, [((i + 1) % count, i) for i in range(ends)]),
            ],
            axis=dim,
        )
    return cells


def from_partner(x, axis, stride):
    return lax.ppermute(x, axis, [(i, i ^ 1 << stride) for i in range(lax.axis_size(axis))])


def make_taps(extended, rows, width):
    pieces = [extended[:, dy : dy + rows, dx : dx + width, :] for dy in range(3) for dx in range(3)]
    stacked = jnp.stack(pieces, axis=3)
    count = stacked.shape[0] * rows * width
    return stacked.reshape(count, 9, stacked.shape[-1])


def load_adapter_factors(
    adapter_down_weight, adapter_up_weight, request_adapter, adapter_row_table, request_total
):
    resident_count = adapter_down_weight.shape[0]
    fetched = []
    for request in range(request_total):
        resident_row = adapter_row_table[request_adapter[request]]
        owner = resident_row // resident_count
        store_position = resident_row % resident_count
        resident_down = lax.dynamic_index_in_dim(
            adapter_down_weight, store_position, 0, keepdims=False
        )
        resident_up = lax.dynamic_index_in_dim(adapter_up_weight, store_position, 0, keepdims=False)
        fetched.append(
            (broadcast(resident_down, "patch", owner), broadcast(resident_up, "patch", owner))
        )
    return fetched


def shards(
    hidden,
    skip,
    timestep_embedding_table,
    timesteps,
    group_norm_gain,
    group_norm_bias,
    kernel_weight,
    adapter_down_weight,
    adapter_up_weight,
    request_adapter,
    adapter_row_table,
):
    request_total, rows, width, chans = hidden.shape
    steps_count = timestep_embedding_table.shape[0]
    onehot = (timesteps[:, None] == jnp.arange(steps_count, dtype=jnp.int32)[None, :]).astype(
        jnp.float32
    )
    temb = jnp.dot(
        onehot,
        timestep_embedding_table,
        preferred_element_type=jnp.float32,
        precision=lax.Precision.HIGHEST,
    )
    shifted = hidden + temb[:, None, None, :]
    grouped = shifted.reshape(request_total, rows, width, GROUPS, chans // GROUPS)
    count = rows * lax.axis_size("patch") * width * (chans // GROUPS)
    totals = lax.psum(jnp.sum(grouped, axis=(1, 2, 4)), "patch")
    mean = totals / count
    centered = grouped - mean[:, None, None, :, None]
    squares = lax.psum(jnp.sum(centered * centered, axis=(1, 2, 4)), "patch")
    var = squares / count
    normed = (centered * lax.rsqrt(var + 1e-05)[:, None, None, :, None]).reshape(
        request_total, rows, width, chans
    )
    act = jax.nn.silu(normed * group_norm_gain + group_norm_bias).astype(jnp.bfloat16)
    extended = padded(act, (("patch", 1),), 1)
    extended = jnp.pad(extended, ((0, 0), (0, 0), (1, 1), (0, 0)))
    partner = from_partner(extended, "req", 0)
    taps = make_taps(jnp.concatenate([extended, partner], axis=0), rows, width)
    pixels = request_total * rows * width
    conv_half = jnp.einsum(
        "ptc,tco->po",
        taps,
        lax.all_gather(kernel_weight, "patch", axis=1, tiled=True),
        preferred_element_type=jnp.float32,
    )
    own_half = conv_half[:pixels]
    returned = from_partner(conv_half[pixels:], "req", 0)
    first = lax.axis_index("req") == 0
    left_half = jnp.where(first, own_half, returned)
    right_half = jnp.where(first, returned, own_half)
    conv = jnp.concatenate([left_half, right_half], axis=1).reshape(
        request_total, rows * width, chans
    )
    own_taps = taps[:pixels].reshape(request_total, rows * width, 9 * chans)
    adapter_factors = load_adapter_factors(
        adapter_down_weight, adapter_up_weight, request_adapter, adapter_row_table, request_total
    )
    deltas = []
    for request in range(request_total):
        down_factor, upper_limit = adapter_factors[request]
        low = lax.dot_general(
            own_taps[request],
            down_factor,
            (((1,), (1,)), ((), ())),
            preferred_element_type=jnp.float32,
        ).astype(jnp.bfloat16)
        deltas.append(jnp.dot(low, upper_limit, preferred_element_type=jnp.float32))
    total = conv + jnp.stack(deltas, axis=0)
    return skip + total.reshape(request_total, rows, width, chans)


def solution(mesh):
    def step(*args):
        n = lax.axis_size("patch")
        if fits(n, args[0], args[6], args[7]):
            return split_contraction(*args)
        return shards(*args)

    return jax.shard_map(
        step,
        mesh=mesh,
        in_specs=(
            P(("groups", "req"), "patch", None, None),
            P(("groups", "req"), "patch", None, None),
            P(),
            P(("groups", "req")),
            P(),
            P(),
            P(None, "patch", "req"),
            P(("groups", "patch"), None, None),
            P(("groups", "patch"), None, None),
            P(("groups", "req")),
            P("groups"),
        ),
        out_specs=P(("groups", "req"), "patch", None, None),
        check_vma=False,
    )
```

```python
import functools

import jax
import jax.numpy as jnp
from jax import lax
from jax.experimental import pallas as pl
from jax.experimental.pallas import tpu as pltpu
from jax.sharding import PartitionSpec as P

GROUPS = 32
LANES = 128
WIN = 256
MESH = pl.DeviceIdType.MESH
BF = jnp.bfloat16
F32 = jnp.float32


def hi_dot(a, b, dims):
    return lax.dot_general(
        a, b, (dims, ((), ())), precision=lax.Precision.HIGHEST, preferred_element_type=F32
    )


def block_kernel(
    n, own, reqs, width, chans,
    steps, asked, row_of, hid, skip, table, gain, bias, w_hbm, d_hbm, u_hbm,
    out,
    act, acts_in, taps, wpad, dall, uall, stat_out, stat_in,
    xsend, xrecv, keep, zsend, zrecv, lsend, lrecv,
    st_s, st_r, ac_s, ac_r, ac_l, d_s, d_r, d_l, w_s, w_r, w_l, dp_s, dp_r,
    x_s, x_r, z_s, z_r, l_s, l_r, u_s, u_f, u_r, u_l, up_s, up_r,
):
    me = lax.axis_index("patch")
    core = lax.axis_index("req")
    mate = 1 - core
    zs = n // 2
    z, x = me // 2, me % 2
    half = chans // 2
    rank = dall.shape[1]
    hrank = rank // 2
    per = d_hbm.shape[0]
    temb = [table[pl.ds(steps[r], 1), :] for r in range(reqs)]
    sel = [row_of[asked[r]] for r in range(reqs)]

    def window(j):
        return pl.multiple_of((j * own) // LANES * LANES, LANES)

    wpad[...] = jnp.zeros_like(wpad)

    barrier = pltpu.get_barrier_semaphore()
    for k in range(1, n):
        pl.semaphore_signal(barrier, inc=1, device_id={"patch": (me + k) % n}, device_id_type=MESH)
    pl.semaphore_signal(barrier, inc=1, device_id={"req": mate}, device_id_type=MESH)
    pl.semaphore_wait(barrier, n)

    inner = pl.multiple_of((me * own) % LANES, 32)

    def w_dst(t, c):
        return wpad.at[
            t // 3,
            pl.ds(pl.multiple_of((t % 3) * WIN + inner, 32), own),
            pl.ds(pl.multiple_of(c * half, LANES), half),
        ]

    def w_remote(t, c):
        return pltpu.make_async_remote_copy(
            src_ref=w_hbm.at[t], dst_ref=w_dst(t, c), send_sem=w_s.at[t], recv_sem=w_r.at[t],
            device_id={"req": mate}, device_id_type=MESH,
        )

    def w_local(t):
        return pltpu.make_async_copy(w_hbm.at[t], w_dst(t, core), w_l.at[t])

    for t in range(9):
        w_local(t).start()
        w_remote(t, core).start()

    rank_at = pl.multiple_of(core * hrank, hrank)

    def d_src(t, peer):
        return d_hbm.at[:, pl.ds(rank_at, hrank), pl.ds(pl.multiple_of(t * chans + window(peer), LANES), WIN)]

    def d_dst(t, src):
        return dall.at[pl.ds(src * per, per), pl.ds(rank_at, hrank), pl.ds(pl.multiple_of(t * WIN, WIN), WIN)]

    def d_copy(t, peer, src):
        return pltpu.make_async_remote_copy(
            src_ref=d_src(t, peer), dst_ref=d_dst(t, src),
            send_sem=d_s.at[peer, t], recv_sem=d_r.at[src, t],
            device_id={"patch": peer}, device_id_type=MESH,
        )

    def d_own(t):
        return pltpu.make_async_copy(d_src(t, me), d_dst(t, me), d_l.at[t])

    def send_down(lo, hi):
        @pl.loop(lo, hi)
        def _(t):
            d_own(t).start()

            @pl.loop(1, n)
            def _(k):
                d_copy(t, (me + k) % n, me).start()

    def u_dst(src):
        return uall.at[pl.ds(src * per, per), pl.ds(rank_at, hrank), :]

    near = me + 1 - 2 * x

    def u_copy(peer, src):
        return pltpu.make_async_remote_copy(
            src_ref=u_hbm.at[:, pl.ds(rank_at, hrank), :], dst_ref=u_dst(src),
            send_sem=u_s.at[peer], recv_sem=u_r.at[src],
            device_id={"patch": peer}, device_id_type=MESH,
        )

    def u_pass(src):
        return pltpu.make_async_remote_copy(
            src_ref=u_dst(src), dst_ref=u_dst(src), send_sem=u_f.at[src], recv_sem=u_r.at[src],
            device_id={"patch": near}, device_id_type=MESH,
        )

    u_own = pltpu.make_async_copy(u_hbm.at[:, pl.ds(rank_at, hrank), :], u_dst(me), u_l)

    def send_up():
        u_own.start()
        u_copy(near, me).start()
        for k in range(1, zs):
            u_copy((z + k) % zs * 2 + x, me).start()

    send_down(0, 3)

    c_of = lax.broadcasted_iota(jnp.int32, (chans, LANES), 0)
    g_of = lax.broadcasted_iota(jnp.int32, (chans, LANES), 1)
    size = chans // GROUPS
    member = jnp.where((c_of >= g_of * size) & (c_of < (g_of + 1) * size), 1.0, 0.0).astype(F32)
    count = width * size
    sums = [
        jnp.sum(hid[r * width : (r + 1) * width, :] + temb[r], axis=0, keepdims=True)
        for r in range(reqs)
    ]
    pad = [jnp.zeros((8 - reqs, chans), F32)] if reqs < 8 else []
    mean = hi_dot(jnp.concatenate(sums + pad, axis=0), member, ((1,), (0,))) / count
    wide = hi_dot(mean, member, ((1,), (1,)))
    squares = []
    for r in range(reqs):
        c = hid[r * width : (r + 1) * width, :] + temb[r] - wide[r : r + 1, :]
        squares.append(jnp.sum(c * c, axis=0, keepdims=True))
    second = hi_dot(jnp.concatenate(squares + pad, axis=0), member, ((1,), (0,)))
    stat_out[0] = mean
    stat_out[1] = second

    def st_copy(peer, src):
        return pltpu.make_async_remote_copy(
            src_ref=stat_out, dst_ref=stat_in.at[src], send_sem=st_s.at[peer], recv_sem=st_r.at[src],
            device_id={"patch": peer}, device_id_type=MESH,
        )

    for k in range(1, n):
        st_copy((me + k) % n, me).start()
    stat_in[me] = stat_out[...]
    for k in range(1, n):
        st_copy((me + k) % n, (me + k) % n).wait_recv()
    means = stat_in[:, 0]
    total_mean = jnp.sum(means, axis=0) / n
    spread = means - total_mean[None]
    var = (jnp.sum(stat_in[:, 1], axis=0) + count * jnp.sum(spread * spread, axis=0)) / (count * n)
    mean_w = hi_dot(total_mean, member, ((1,), (1,)))
    inv_w = hi_dot(lax.rsqrt(var + 1e-05), member, ((1,), (1,)))
    for r in range(reqs):
        rows = slice(r * width, (r + 1) * width)
        v = (hid[rows, :] + temb[r] - mean_w[r : r + 1, :]) * inv_w[r : r + 1, :]
        v = v * gain[...] + bias[...]
        act[rows, :] = (v / (1.0 + jnp.exp(-v))).astype(BF)

    def ac_copy(peer, src):
        return pltpu.make_async_remote_copy(
            src_ref=act.at[:, pl.ds(window(peer), WIN)], dst_ref=acts_in.at[src],
            send_sem=ac_s.at[peer], recv_sem=ac_r.at[src],
            device_id={"patch": peer}, device_id_type=MESH,
        )

    ac_own = pltpu.make_async_copy(act.at[:, pl.ds(window(me), WIN)], acts_in.at[me], ac_l)
    for k in range(1, n):
        ac_copy((me + k) % n, me).start()
    ac_own.start()

    send_down(3, 9)
    send_up()

    taps[0] = jnp.zeros(taps.shape[1:], BF)
    taps[n + 1] = jnp.zeros(taps.shape[1:], BF)
    cells = reqs * width
    px = lax.broadcasted_iota(jnp.int32, (cells, WIN), 0) % width
    ch = lax.broadcasted_iota(jnp.int32, (cells, WIN), 1)
    mine = (ch >= inner) & (ch < inner + own)

    def lay(y):
        v = jnp.where(mine, acts_in[y].astype(F32), 0.0)
        taps[y + 1, :, 0:WIN] = jnp.where(px == 0, 0.0, pltpu.roll(v, 1, 0)).astype(BF)
        taps[y + 1, :, WIN : 2 * WIN] = v.astype(BF)
        taps[y + 1, :, 2 * WIN :] = jnp.where(px == width - 1, 0.0, pltpu.roll(v, cells - 1, 0)).astype(BF)

    ac_own.wait()
    lay(me)

    @pl.loop(1, n)
    def _(k):
        y = (me + k) % n
        ac_copy(y, y).wait_recv()
        lay(y)

    for t in range(9):
        w_local(t).wait()
        w_remote(t, mate).wait_recv()

    def conv(y, put):
        @pl.loop(0, chans // WIN)
        def _(m):
            cols = pl.ds(pl.multiple_of(m * WIN, WIN), WIN)
            s = jnp.dot(taps[y], wpad[0, :, cols], preferred_element_type=F32)
            s += jnp.dot(taps[y + 1], wpad[1, :, cols], preferred_element_type=F32)
            s += jnp.dot(taps[y + 2], wpad[2, :, cols], preferred_element_type=F32)
            put(cols, s)

    def x_copy(i):
        return pltpu.make_async_remote_copy(
            src_ref=xsend.at[i], dst_ref=xrecv.at[i], send_sem=x_s.at[i], recv_sem=x_r.at[i],
            device_id={"patch": near}, device_id_type=MESH,
        )

    def z_copy(i, zt, src):
        return pltpu.make_async_remote_copy(
            src_ref=zsend.at[i], dst_ref=zrecv.at[src], send_sem=z_s.at[i], recv_sem=z_r.at[src],
            device_id={"patch": zt * 2 + x}, device_id_type=MESH,
        )

    def forward(i):
        x_copy(i).wait_recv()
        zsend[i] = (keep[i] + xrecv[i].astype(F32)).astype(BF)
        z_copy(i, (z + 1 + i) % zs, z).start()

    @pl.loop(0, zs)
    def _(i):
        def put(cols, s):
            xsend[i, :, cols] = s.astype(BF)

        conv((z + 1 + i) % zs * 2 + 1 - x, put)
        x_copy(i).start()

    @pl.loop(0, zs)
    def _(i):
        def put(cols, s):
            keep[i, :, cols] = s

        conv((z + 1 + i) % zs * 2 + x, put)

    forward(0)

    @pl.loop(0, 9)
    def _(t):
        d_own(t).wait()

        @pl.loop(1, n)
        def _(k):
            d_copy(t, (me + k) % n, (me + k) % n).wait_recv()

    def dp_copy(at):
        part = dall.at[:, pl.ds(pl.multiple_of(at * hrank, hrank), hrank), :]
        return pltpu.make_async_remote_copy(
            src_ref=part, dst_ref=part, send_sem=dp_s, recv_sem=dp_r,
            device_id={"req": mate}, device_id_type=MESH,
        )

    dp_copy(core).start()
    for k in range(1, zs):
        src = (z + k) % zs * 2 + x
        u_copy(src, src).wait_recv()
        u_pass(src).start()
    for i in range(1, zs - 1):
        forward(i)
    dp_copy(mate).wait_recv()
    for q in range(reqs // 2):
        pair = []
        for r in (2 * q, 2 * q + 1):
            factor = dall[sel[r]]
            low = jnp.zeros((n * width, rank), F32)
            for dy in range(3):
                lhs = taps[dy : dy + n, r * width : (r + 1) * width, :].reshape(n * width, 3 * WIN)
                low += lax.dot_general(
                    lhs, factor[:, dy * 3 * WIN : (dy + 1) * 3 * WIN], (((1,), (1,)), ((), ())),
                    preferred_element_type=F32,
                )
            pair.append(low)
        both = jnp.concatenate(pair, axis=1).astype(BF)
        lsend[:, q * width : (q + 1) * width, :] = both.reshape(n, width, 2 * rank)

    def l_copy(peer, src):
        return pltpu.make_async_remote_copy(
            src_ref=lsend.at[peer], dst_ref=lrecv.at[src], send_sem=l_s.at[peer], recv_sem=l_r.at[src],
            device_id={"patch": peer}, device_id_type=MESH,
        )

    for k in range(1, n):
        l_copy((me + k) % n, me).start()

    u_own.wait()
    u_copy(near, near).wait_recv()
    for k in range(1, zs):
        u_pass((z + k) % zs * 2 + 1 - x).wait_recv()

    def up_copy(at):
        part = uall.at[:, pl.ds(pl.multiple_of(at * hrank, hrank), hrank), :]
        return pltpu.make_async_remote_copy(
            src_ref=part, dst_ref=part, send_sem=up_s, recv_sem=up_r,
            device_id={"req": mate}, device_id_type=MESH,
        )

    up_copy(core).start()
    x_copy(zs - 1).wait_recv()
    out[...] = skip[...] + keep[zs - 1] + xrecv[zs - 1].astype(F32)
    for k in range(1, zs):
        src = (z + k) % zs
        z_copy(0, src, src).wait_recv()
        out[...] += zrecv[src].astype(F32)
    up_copy(mate).wait_recv()
    both = lsend[me].astype(F32)
    for k in range(1, n):
        src = (me + k) % n
        l_copy(src, src).wait_recv()
        both += lrecv[src].astype(F32)
    both = both.astype(BF)
    for r in range(reqs):
        low = both[r // 2 * width : (r // 2 + 1) * width, r % 2 * rank : (r % 2 + 1) * rank]
        out[r * width : (r + 1) * width, :] += jnp.dot(low, uall[sel[r]], preferred_element_type=F32)

    dp_copy(core).wait_send()
    up_copy(core).wait_send()
    u_copy(near, me).wait_send()
    for k in range(1, zs):
        u_copy((z + k) % zs * 2 + x, me).wait_send()
        u_pass((z + k) % zs * 2 + x).wait_send()
    for t in range(9):
        w_remote(t, core).wait_send()
    for k in range(1, n):
        st_copy((me + k) % n, me).wait_send()
        ac_copy((me + k) % n, me).wait_send()
        l_copy((me + k) % n, me).wait_send()

    @pl.loop(0, 9)
    def _(t):
        @pl.loop(1, n)
        def _(k):
            d_copy(t, (me + k) % n, me).wait_send()

    @pl.loop(0, zs)
    def _(i):
        x_copy(i).wait_send()

    @pl.loop(0, zs - 1)
    def _(i):
        z_copy(i, (z + 1 + i) % zs, z).wait_send()


def run_block(n, steps, asked, row_of, hid, skip, table, gain, bias, weight, down, up):
    cells, chans = hid.shape
    reqs = asked.shape[0]
    width = cells // reqs
    own = weight.shape[1]
    per, rank, _ = down.shape
    zs = n // 2
    dma = pltpu.SemaphoreType.DMA
    vmem = pl.BlockSpec(memory_space=pltpu.VMEM)
    hbm = pl.BlockSpec(memory_space=pl.ANY)
    smem = pl.BlockSpec(memory_space=pltpu.SMEM)
    return pl.pallas_call(
        functools.partial(block_kernel, n, own, reqs, width, chans),
        out_shape=jax.ShapeDtypeStruct((cells, chans), F32),
        in_specs=[smem] * 3 + [vmem] * 5 + [hbm] * 3,
        out_specs=vmem,
        scratch_shapes=[
            pltpu.VMEM((cells, chans), BF),
            pltpu.VMEM((n, cells, WIN), BF),
            pltpu.VMEM((n + 2, cells, 3 * WIN), BF),
            pltpu.VMEM((3, 3 * WIN, chans), BF),
            pltpu.VMEM((n * per, rank, 9 * WIN), BF),
            pltpu.VMEM((n * per, rank, chans), BF),
            pltpu.VMEM((2, 8, LANES), F32),
            pltpu.VMEM((n, 2, 8, LANES), F32),
            pltpu.VMEM((zs, cells, chans), BF),
            pltpu.VMEM((zs, cells, chans), BF),
            pltpu.VMEM((zs, cells, chans), F32),
            pltpu.VMEM((zs - 1, cells, chans), BF),
            pltpu.VMEM((zs, cells, chans), BF),
            pltpu.VMEM((n, cells // 2, 2 * rank), BF),
            pltpu.VMEM((n, cells // 2, 2 * rank), BF),
            dma((n,)), dma((n,)),
            dma((n,)), dma((n,)), dma,
            dma((n, 9)), dma((n, 9)), dma((9,)),
            dma((9,)), dma((9,)), dma((9,)),
            dma, dma,
            dma((zs,)), dma((zs,)),
            dma((zs - 1,)), dma((zs,)),
            dma((n,)), dma((n,)),
            dma((n,)), dma((n,)), dma((n,)), dma,
            dma, dma,
        ],
        compiler_params=pltpu.CompilerParams(
            collective_id=0, has_side_effects=True, vmem_limit_bytes=56 * 2**20
        ),
        cost_estimate=pl.CostEstimate(
            flops=2 * n * cells * 9 * WIN * chans, bytes_accessed=10**8, transcendentals=0
        ),
    )(steps, asked, row_of, hid, skip, table, gain, bias, weight, down, up)


def split_contraction(
    hidden, skip, timestep_embedding_table, timesteps, group_norm_gain, group_norm_bias,
    kernel_weight, adapter_down_weight, adapter_up_weight, request_adapter, adapter_row_table,
):
    shape = hidden.shape
    flat = (shape[0] * shape[1] * shape[2], shape[3])
    return run_block(
        lax.axis_size("patch"), timesteps, request_adapter, adapter_row_table,
        hidden.reshape(flat), skip.reshape(flat), timestep_embedding_table,
        group_norm_gain[None], group_norm_bias[None],
        kernel_weight, adapter_down_weight, adapter_up_weight,
    ).reshape(shape)


def fits(n, hidden, kernel_weight, down):
    own = kernel_weight.shape[1]
    ends = all(j * own // LANES * LANES + WIN <= hidden.shape[3] and j * own % LANES + own <= WIN for j in range(n))
    return (
        n % 2 == 0 and n <= 8 and hidden.shape[1] == 1 and hidden.shape[0] in (2, 4, 6, 8)
        and own % 32 == 0 and ends and down.shape[1] == 64
    )


def broadcast(block, axis, owner):
    block = jnp.where(lax.axis_index(axis) == owner, block, jnp.zeros_like(block))
    return lax.psum(block, axis)


def padded(cells, sides, width):
    for axis, dim in sides:
        count = lax.axis_size(axis)
        ends = count - 1
        head = lax.slice_in_dim(cells, 0, width, axis=dim)
        tail = lax.slice_in_dim(cells, cells.shape[dim] - width, cells.shape[dim], axis=dim)
        cells = jnp.concatenate(
            [
                lax.ppermute(tail, axis, [(i, (i + 1) % count) for i in range(ends)]),
                cells,
                lax.ppermute(head, axis, [((i + 1) % count, i) for i in range(ends)]),
            ],
            axis=dim,
        )
    return cells


def from_partner(x, axis, stride):
    return lax.ppermute(x, axis, [(i, i ^ 1 << stride) for i in range(lax.axis_size(axis))])


def make_taps(extended, rows, width):
    pieces = [extended[:, dy : dy + rows, dx : dx + width, :] for dy in range(3) for dx in range(3)]
    stacked = jnp.stack(pieces, axis=3)
    count = stacked.shape[0] * rows * width
    return stacked.reshape(count, 9, stacked.shape[-1])


def load_adapter_factors(
    adapter_down_weight, adapter_up_weight, request_adapter, adapter_row_table, request_total
):
    resident_count = adapter_down_weight.shape[0]
    fetched = []
    for request in range(request_total):
        resident_row = adapter_row_table[request_adapter[request]]
        owner = resident_row // resident_count
        store_position = resident_row % resident_count
        resident_down = lax.dynamic_index_in_dim(
            adapter_down_weight, store_position, 0, keepdims=False
        )
        resident_up = lax.dynamic_index_in_dim(adapter_up_weight, store_position, 0, keepdims=False)
        fetched.append(
            (broadcast(resident_down, "patch", owner), broadcast(resident_up, "patch", owner))
        )
    return fetched


def shards(
    hidden,
    skip,
    timestep_embedding_table,
    timesteps,
    group_norm_gain,
    group_norm_bias,
    kernel_weight,
    adapter_down_weight,
    adapter_up_weight,
    request_adapter,
    adapter_row_table,
):
    request_total, rows, width, chans = hidden.shape
    steps_count = timestep_embedding_table.shape[0]
    onehot = (timesteps[:, None] == jnp.arange(steps_count, dtype=jnp.int32)[None, :]).astype(
        jnp.float32
    )
    temb = jnp.dot(
        onehot,
        timestep_embedding_table,
        preferred_element_type=jnp.float32,
        precision=lax.Precision.HIGHEST,
    )
    shifted = hidden + temb[:, None, None, :]
    grouped = shifted.reshape(request_total, rows, width, GROUPS, chans // GROUPS)
    count = rows * lax.axis_size("patch") * width * (chans // GROUPS)
    totals = lax.psum(jnp.sum(grouped, axis=(1, 2, 4)), "patch")
    mean = totals / count
    centered = grouped - mean[:, None, None, :, None]
    squares = lax.psum(jnp.sum(centered * centered, axis=(1, 2, 4)), "patch")
    var = squares / count
    normed = (centered * lax.rsqrt(var + 1e-05)[:, None, None, :, None]).reshape(
        request_total, rows, width, chans
    )
    act = jax.nn.silu(normed * group_norm_gain + group_norm_bias).astype(jnp.bfloat16)
    extended = padded(act, (("patch", 1),), 1)
    extended = jnp.pad(extended, ((0, 0), (0, 0), (1, 1), (0, 0)))
    partner = from_partner(extended, "req", 0)
    taps = make_taps(jnp.concatenate([extended, partner], axis=0), rows, width)
    pixels = request_total * rows * width
    conv_half = jnp.einsum(
        "ptc,tco->po",
        taps,
        lax.all_gather(kernel_weight, "patch", axis=1, tiled=True),
        preferred_element_type=jnp.float32,
    )
    own_half = conv_half[:pixels]
    returned = from_partner(conv_half[pixels:], "req", 0)
    first = lax.axis_index("req") == 0
    left_half = jnp.where(first, own_half, returned)
    right_half = jnp.where(first, returned, own_half)
    conv = jnp.concatenate([left_half, right_half], axis=1).reshape(
        request_total, rows * width, chans
    )
    own_taps = taps[:pixels].reshape(request_total, rows * width, 9 * chans)
    adapter_factors = load_adapter_factors(
        adapter_down_weight, adapter_up_weight, request_adapter, adapter_row_table, request_total
    )
    deltas = []
    for request in range(request_total):
        down_factor, upper_limit = adapter_factors[request]
        low = lax.dot_general(
            own_taps[request],
            down_factor,
            (((1,), (1,)), ((), ())),
            preferred_element_type=jnp.float32,
        ).astype(jnp.bfloat16)
        deltas.append(jnp.dot(low, upper_limit, preferred_element_type=jnp.float32))
    total = conv + jnp.stack(deltas, axis=0)
    return skip + total.reshape(request_total, rows, width, chans)


def solution(mesh):
    def step(*args):
        n = lax.axis_size("patch")
        if fits(n, args[0], args[6], args[7]):
            return split_contraction(*args)
        return shards(*args)

    return jax.shard_map(
        step,
        mesh=mesh,
        in_specs=(
            P(("groups", "req"), "patch", None, None),
            P(("groups", "req"), "patch", None, None),
            P(),
            P(("groups", "req")),
            P(),
            P(),
            P(None, "patch", "req"),
            P(("groups", "patch"), None, None),
            P(("groups", "patch"), None, None),
            P(("groups", "req")),
            P("groups"),
        ),
        out_specs=P(("groups", "req"), "patch", None, None),
        check_vma=False,
    )
```

```python
import functools

import jax
import jax.numpy as jnp
from jax import lax
from jax.experimental import pallas as pl
from jax.experimental.pallas import tpu as pltpu
from jax.sharding import PartitionSpec as P

GROUPS = 32
LANES = 128
WIN = 256
MESH = pl.DeviceIdType.MESH
BF = jnp.bfloat16
F32 = jnp.float32


def hi_dot(a, b, dims):
    return lax.dot_general(
        a, b, (dims, ((), ())), precision=lax.Precision.HIGHEST, preferred_element_type=F32
    )


def block_kernel(
    n, own, reqs, width, chans,
    steps, asked, row_of, hid, skip, table, gain, bias, w_hbm, d_hbm, u_hbm,
    out,
    act, acts_in, taps, wpad, dall, uall, stat_out, stat_in,
    xsend, xrecv, keep, zsend, zrecv, lsend, lrecv,
    st_s, st_r, ac_s, ac_r, ac_l, d_s, d_r, d_l, w_s, w_r, w_l, dp_s, dp_r,
    x_s, x_r, z_s, z_r, l_s, l_r, u_s, u_f, u_r, u_l, up_s, up_r,
):
    me = lax.axis_index("patch")
    core = lax.axis_index("req")
    mate = 1 - core
    zs = n // 2
    z, x = me // 2, me % 2
    half = chans // 2
    rank = dall.shape[1]
    hrank = rank // 2
    per = d_hbm.shape[0]
    temb = [table[pl.ds(steps[r], 1), :] for r in range(reqs)]
    sel = [row_of[asked[r]] for r in range(reqs)]

    def window(j):
        return pl.multiple_of((j * own) // LANES * LANES, LANES)

    wpad[...] = jnp.zeros_like(wpad)

    barrier = pltpu.get_barrier_semaphore()
    for k in range(1, n):
        pl.semaphore_signal(barrier, inc=1, device_id={"patch": (me + k) % n}, device_id_type=MESH)
    pl.semaphore_signal(barrier, inc=1, device_id={"req": mate}, device_id_type=MESH)
    pl.semaphore_wait(barrier, n)

    inner = pl.multiple_of((me * own) % LANES, 32)

    def w_dst(t, c):
        return wpad.at[
            t // 3,
            pl.ds(pl.multiple_of((t % 3) * WIN + inner, 32), own),
            pl.ds(pl.multiple_of(c * half, LANES), half),
        ]

    def w_remote(t, c):
        return pltpu.make_async_remote_copy(
            src_ref=w_hbm.at[t], dst_ref=w_dst(t, c), send_sem=w_s.at[t], recv_sem=w_r.at[t],
            device_id={"req": mate}, device_id_type=MESH,
        )

    def w_local(t):
        return pltpu.make_async_copy(w_hbm.at[t], w_dst(t, core), w_l.at[t])

    for t in range(9):
        w_local(t).start()
        w_remote(t, core).start()

    rank_at = pl.multiple_of(core * hrank, hrank)

    def d_src(t, peer):
        return d_hbm.at[:, pl.ds(rank_at, hrank), pl.ds(pl.multiple_of(t * chans + window(peer), LANES), WIN)]

    def d_dst(t, src):
        return dall.at[pl.ds(src * per, per), pl.ds(rank_at, hrank), pl.ds(pl.multiple_of(t * WIN, WIN), WIN)]

    def d_copy(t, peer, src):
        return pltpu.make_async_remote_copy(
            src_ref=d_src(t, peer), dst_ref=d_dst(t, src),
            send_sem=d_s.at[peer, t], recv_sem=d_r.at[src, t],
            device_id={"patch": peer}, device_id_type=MESH,
        )

    def d_own(t):
        return pltpu.make_async_copy(d_src(t, me), d_dst(t, me), d_l.at[t])

    def send_down(lo, hi):
        @pl.loop(lo, hi)
        def _(t):
            d_own(t).start()

            @pl.loop(1, n)
            def _(k):
                d_copy(t, (me + k) % n, me).start()

    def u_dst(src):
        return uall.at[pl.ds(src * per, per), pl.ds(rank_at, hrank), :]

    near = me + 1 - 2 * x

    def u_copy(peer, src):
        return pltpu.make_async_remote_copy(
            src_ref=u_hbm.at[:, pl.ds(rank_at, hrank), :], dst_ref=u_dst(src),
            send_sem=u_s.at[peer], recv_sem=u_r.at[src],
            device_id={"patch": peer}, device_id_type=MESH,
        )

    def u_pass(src):
        return pltpu.make_async_remote_copy(
            src_ref=u_dst(src), dst_ref=u_dst(src), send_sem=u_f.at[src], recv_sem=u_r.at[src],
            device_id={"patch": near}, device_id_type=MESH,
        )

    u_own = pltpu.make_async_copy(u_hbm.at[:, pl.ds(rank_at, hrank), :], u_dst(me), u_l)

    def send_up():
        u_own.start()
        u_copy(near, me).start()
        for k in range(1, zs):
            u_copy((z + k) % zs * 2 + x, me).start()

    send_down(0, 3)

    c_of = lax.broadcasted_iota(jnp.int32, (chans, LANES), 0)
    g_of = lax.broadcasted_iota(jnp.int32, (chans, LANES), 1)
    size = chans // GROUPS
    member = jnp.where((c_of >= g_of * size) & (c_of < (g_of + 1) * size), 1.0, 0.0).astype(F32)
    count = width * size
    sums = [
        jnp.sum(hid[r * width : (r + 1) * width, :] + temb[r], axis=0, keepdims=True)
        for r in range(reqs)
    ]
    pad = [jnp.zeros((8 - reqs, chans), F32)] if reqs < 8 else []
    mean = hi_dot(jnp.concatenate(sums + pad, axis=0), member, ((1,), (0,))) / count
    wide = hi_dot(mean, member, ((1,), (1,)))
    squares = []
    for r in range(reqs):
        c = hid[r * width : (r + 1) * width, :] + temb[r] - wide[r : r + 1, :]
        squares.append(jnp.sum(c * c, axis=0, keepdims=True))
    second = hi_dot(jnp.concatenate(squares + pad, axis=0), member, ((1,), (0,)))
    stat_out[0] = mean
    stat_out[1] = second

    def st_copy(peer, src):
        return pltpu.make_async_remote_copy(
            src_ref=stat_out, dst_ref=stat_in.at[src], send_sem=st_s.at[peer], recv_sem=st_r.at[src],
            device_id={"patch": peer}, device_id_type=MESH,
        )

    for k in range(1, n):
        st_copy((me + k) % n, me).start()
    stat_in[me] = stat_out[...]
    for k in range(1, n):
        st_copy((me + k) % n, (me + k) % n).wait_recv()
    means = stat_in[:, 0]
    total_mean = jnp.sum(means, axis=0) / n
    spread = means - total_mean[None]
    var = (jnp.sum(stat_in[:, 1], axis=0) + count * jnp.sum(spread * spread, axis=0)) / (count * n)
    mean_w = hi_dot(total_mean, member, ((1,), (1,)))
    inv_w = hi_dot(lax.rsqrt(var + 1e-05), member, ((1,), (1,)))
    for r in range(reqs):
        rows = slice(r * width, (r + 1) * width)
        v = (hid[rows, :] + temb[r] - mean_w[r : r + 1, :]) * inv_w[r : r + 1, :]
        v = v * gain[...] + bias[...]
        act[rows, :] = (v / (1.0 + jnp.exp(-v))).astype(BF)

    def ac_copy(peer, src):
        return pltpu.make_async_remote_copy(
            src_ref=act.at[:, pl.ds(window(peer), WIN)], dst_ref=acts_in.at[src],
            send_sem=ac_s.at[peer], recv_sem=ac_r.at[src],
            device_id={"patch": peer}, device_id_type=MESH,
        )

    ac_own = pltpu.make_async_copy(act.at[:, pl.ds(window(me), WIN)], acts_in.at[me], ac_l)
    for k in range(1, n):
        ac_copy((me + k) % n, me).start()
    ac_own.start()

    send_down(3, 9)
    send_up()

    taps[0] = jnp.zeros(taps.shape[1:], BF)
    taps[n + 1] = jnp.zeros(taps.shape[1:], BF)
    cells = reqs * width
    px = lax.broadcasted_iota(jnp.int32, (cells, WIN), 0) % width
    ch = lax.broadcasted_iota(jnp.int32, (cells, WIN), 1)
    mine = (ch >= inner) & (ch < inner + own)

    def lay(y):
        v = jnp.where(mine, acts_in[y].astype(F32), 0.0)
        taps[y + 1, :, 0:WIN] = jnp.where(px == 0, 0.0, pltpu.roll(v, 1, 0)).astype(BF)
        taps[y + 1, :, WIN : 2 * WIN] = v.astype(BF)
        taps[y + 1, :, 2 * WIN :] = jnp.where(px == width - 1, 0.0, pltpu.roll(v, cells - 1, 0)).astype(BF)

    ac_own.wait()
    lay(me)

    @pl.loop(1, n)
    def _(k):
        y = (me + k) % n
        ac_copy(y, y).wait_recv()
        lay(y)

    for t in range(9):
        w_local(t).wait()
        w_remote(t, mate).wait_recv()

    def conv(y, put):
        @pl.loop(0, chans // WIN)
        def _(m):
            cols = pl.ds(pl.multiple_of(m * WIN, WIN), WIN)
            s = jnp.dot(taps[y], wpad[0, :, cols], preferred_element_type=F32)
            s += jnp.dot(taps[y + 1], wpad[1, :, cols], preferred_element_type=F32)
            s += jnp.dot(taps[y + 2], wpad[2, :, cols], preferred_element_type=F32)
            put(cols, s)

    def x_copy(i):
        return pltpu.make_async_remote_copy(
            src_ref=xsend.at[i], dst_ref=xrecv.at[i], send_sem=x_s.at[i], recv_sem=x_r.at[i],
            device_id={"patch": near}, device_id_type=MESH,
        )

    order = (3 * (1 - z // 2), (2 + 3 * z) % 5, 1 + z % 2, z)

    def z_copy(dest):
        up = dest > z
        after = jnp.where(up, z + 1, z - 1)
        slot = jnp.where(jnp.logical_and(dest < z, after == dest), zs, dest)
        return pltpu.make_async_remote_copy(
            src_ref=zsend.at[dest], dst_ref=zrecv.at[slot], send_sem=z_s.at[dest], recv_sem=z_r.at[slot],
            device_id={"patch": after * 2 + x}, device_id_type=MESH,
        )

    def z_arrival(slot):
        return pltpu.make_async_copy(zrecv.at[slot], zrecv.at[slot], z_r.at[slot])

    def forward(i):
        dest = order[i]
        x_copy(i).wait_recv()
        upward = jnp.logical_and(dest > z, z > 0)
        downward = jnp.logical_and(dest < z, z < zs - 1)

        @pl.when(jnp.logical_or(upward, downward))
        def _():
            z_arrival(dest).wait()
            keep[i] += zrecv[dest].astype(F32)

        zsend[dest] = (keep[i] + xrecv[i].astype(F32)).astype(BF)
        z_copy(dest).start()

    for i in range(zs):
        def put(cols, s, i=i):
            xsend[i, :, cols] = s.astype(BF)

        conv(order[i] * 2 + 1 - x, put)
        x_copy(i).start()

    for i in range(zs):
        def put(cols, s, i=i):
            keep[i, :, cols] = s

        conv(order[i] * 2 + x, put)

    for i in range(zs - 1):
        forward(i)

    @pl.loop(0, 9)
    def _(t):
        d_own(t).wait()

        @pl.loop(1, n)
        def _(k):
            d_copy(t, (me + k) % n, (me + k) % n).wait_recv()

    def dp_copy(at):
        part = dall.at[:, pl.ds(pl.multiple_of(at * hrank, hrank), hrank), :]
        return pltpu.make_async_remote_copy(
            src_ref=part, dst_ref=part, send_sem=dp_s, recv_sem=dp_r,
            device_id={"req": mate}, device_id_type=MESH,
        )

    dp_copy(core).start()
    for k in range(1, zs):
        src = (z + k) % zs * 2 + x
        u_copy(src, src).wait_recv()
        u_pass(src).start()
    dp_copy(mate).wait_recv()
    for q in range(reqs // 2):
        pair = []
        for r in (2 * q, 2 * q + 1):
            factor = dall[sel[r]]
            low = jnp.zeros((n * width, rank), F32)
            for dy in range(3):
                lhs = taps[dy : dy + n, r * width : (r + 1) * width, :].reshape(n * width, 3 * WIN)
                low += lax.dot_general(
                    lhs, factor[:, dy * 3 * WIN : (dy + 1) * 3 * WIN], (((1,), (1,)), ((), ())),
                    preferred_element_type=F32,
                )
            pair.append(low)
        both = jnp.concatenate(pair, axis=1).astype(BF)
        lsend[:, q * width : (q + 1) * width, :] = both.reshape(n, width, 2 * rank)

    def l_copy(peer, src):
        return pltpu.make_async_remote_copy(
            src_ref=lsend.at[peer], dst_ref=lrecv.at[src], send_sem=l_s.at[peer], recv_sem=l_r.at[src],
            device_id={"patch": peer}, device_id_type=MESH,
        )

    for k in range(1, n):
        l_copy((me + k) % n, me).start()

    u_own.wait()
    u_copy(near, near).wait_recv()
    for k in range(1, zs):
        u_pass((z + k) % zs * 2 + 1 - x).wait_recv()

    def up_copy(at):
        part = uall.at[:, pl.ds(pl.multiple_of(at * hrank, hrank), hrank), :]
        return pltpu.make_async_remote_copy(
            src_ref=part, dst_ref=part, send_sem=up_s, recv_sem=up_r,
            device_id={"req": mate}, device_id_type=MESH,
        )

    up_copy(core).start()
    x_copy(zs - 1).wait_recv()
    out[...] = skip[...] + keep[zs - 1] + xrecv[zs - 1].astype(F32)

    @pl.when(z > 0)
    def _():
        z_arrival(z).wait()
        out[...] += zrecv[z].astype(F32)

    @pl.when(z < zs - 1)
    def _():
        z_arrival(zs).wait()
        out[...] += zrecv[zs].astype(F32)

    up_copy(mate).wait_recv()
    both = lsend[me].astype(F32)
    for k in range(1, n):
        src = (me + k) % n
        l_copy(src, src).wait_recv()
        both += lrecv[src].astype(F32)
    both = both.astype(BF)
    for r in range(reqs):
        low = both[r // 2 * width : (r // 2 + 1) * width, r % 2 * rank : (r % 2 + 1) * rank]
        out[r * width : (r + 1) * width, :] += jnp.dot(low, uall[sel[r]], preferred_element_type=F32)

    dp_copy(core).wait_send()
    up_copy(core).wait_send()
    u_copy(near, me).wait_send()
    for k in range(1, zs):
        u_copy((z + k) % zs * 2 + x, me).wait_send()
        u_pass((z + k) % zs * 2 + x).wait_send()
    for t in range(9):
        w_remote(t, core).wait_send()
    for k in range(1, n):
        st_copy((me + k) % n, me).wait_send()
        ac_copy((me + k) % n, me).wait_send()
        l_copy((me + k) % n, me).wait_send()

    @pl.loop(0, 9)
    def _(t):
        @pl.loop(1, n)
        def _(k):
            d_copy(t, (me + k) % n, me).wait_send()

    @pl.loop(0, zs)
    def _(i):
        x_copy(i).wait_send()

    for i in range(zs - 1):
        z_copy(order[i]).wait_send()


def run_block(n, steps, asked, row_of, hid, skip, table, gain, bias, weight, down, up):
    cells, chans = hid.shape
    reqs = asked.shape[0]
    width = cells // reqs
    own = weight.shape[1]
    per, rank, _ = down.shape
    zs = n // 2
    dma = pltpu.SemaphoreType.DMA
    vmem = pl.BlockSpec(memory_space=pltpu.VMEM)
    hbm = pl.BlockSpec(memory_space=pl.ANY)
    smem = pl.BlockSpec(memory_space=pltpu.SMEM)
    return pl.pallas_call(
        functools.partial(block_kernel, n, own, reqs, width, chans),
        out_shape=jax.ShapeDtypeStruct((cells, chans), F32),
        in_specs=[smem] * 3 + [vmem] * 5 + [hbm] * 3,
        out_specs=vmem,
        scratch_shapes=[
            pltpu.VMEM((cells, chans), BF),
            pltpu.VMEM((n, cells, WIN), BF),
            pltpu.VMEM((n + 2, cells, 3 * WIN), BF),
            pltpu.VMEM((3, 3 * WIN, chans), BF),
            pltpu.VMEM((n * per, rank, 9 * WIN), BF),
            pltpu.VMEM((n * per, rank, chans), BF),
            pltpu.VMEM((2, 8, LANES), F32),
            pltpu.VMEM((n, 2, 8, LANES), F32),
            pltpu.VMEM((zs, cells, chans), BF),
            pltpu.VMEM((zs, cells, chans), BF),
            pltpu.VMEM((zs, cells, chans), F32),
            pltpu.VMEM((zs, cells, chans), BF),
            pltpu.VMEM((zs + 1, cells, chans), BF),
            pltpu.VMEM((n, cells // 2, 2 * rank), BF),
            pltpu.VMEM((n, cells // 2, 2 * rank), BF),
            dma((n,)), dma((n,)),
            dma((n,)), dma((n,)), dma,
            dma((n, 9)), dma((n, 9)), dma((9,)),
            dma((9,)), dma((9,)), dma((9,)),
            dma, dma,
            dma((zs,)), dma((zs,)),
            dma((zs,)), dma((zs + 1,)),
            dma((n,)), dma((n,)),
            dma((n,)), dma((n,)), dma((n,)), dma,
            dma, dma,
        ],
        compiler_params=pltpu.CompilerParams(
            collective_id=0, has_side_effects=True, vmem_limit_bytes=56 * 2**20
        ),
        cost_estimate=pl.CostEstimate(
            flops=2 * n * cells * 9 * WIN * chans, bytes_accessed=10**8, transcendentals=0
        ),
    )(steps, asked, row_of, hid, skip, table, gain, bias, weight, down, up)


def split_contraction(
    hidden, skip, timestep_embedding_table, timesteps, group_norm_gain, group_norm_bias,
    kernel_weight, adapter_down_weight, adapter_up_weight, request_adapter, adapter_row_table,
):
    shape = hidden.shape
    flat = (shape[0] * shape[1] * shape[2], shape[3])
    return run_block(
        lax.axis_size("patch"), timesteps, request_adapter, adapter_row_table,
        hidden.reshape(flat), skip.reshape(flat), timestep_embedding_table,
        group_norm_gain[None], group_norm_bias[None],
        kernel_weight, adapter_down_weight, adapter_up_weight,
    ).reshape(shape)


def fits(n, hidden, kernel_weight, down):
    own = kernel_weight.shape[1]
    ends = all(j * own // LANES * LANES + WIN <= hidden.shape[3] and j * own % LANES + own <= WIN for j in range(n))
    return (
        n == 8 and hidden.shape[1] == 1 and hidden.shape[0] in (2, 4, 6, 8)
        and own % 32 == 0 and ends and down.shape[1] == 64
    )


def broadcast(block, axis, owner):
    block = jnp.where(lax.axis_index(axis) == owner, block, jnp.zeros_like(block))
    return lax.psum(block, axis)


def padded(cells, sides, width):
    for axis, dim in sides:
        count = lax.axis_size(axis)
        ends = count - 1
        head = lax.slice_in_dim(cells, 0, width, axis=dim)
        tail = lax.slice_in_dim(cells, cells.shape[dim] - width, cells.shape[dim], axis=dim)
        cells = jnp.concatenate(
            [
                lax.ppermute(tail, axis, [(i, (i + 1) % count) for i in range(ends)]),
                cells,
                lax.ppermute(head, axis, [((i + 1) % count, i) for i in range(ends)]),
            ],
            axis=dim,
        )
    return cells


def from_partner(x, axis, stride):
    return lax.ppermute(x, axis, [(i, i ^ 1 << stride) for i in range(lax.axis_size(axis))])


def make_taps(extended, rows, width):
    pieces = [extended[:, dy : dy + rows, dx : dx + width, :] for dy in range(3) for dx in range(3)]
    stacked = jnp.stack(pieces, axis=3)
    count = stacked.shape[0] * rows * width
    return stacked.reshape(count, 9, stacked.shape[-1])


def load_adapter_factors(
    adapter_down_weight, adapter_up_weight, request_adapter, adapter_row_table, request_total
):
    resident_count = adapter_down_weight.shape[0]
    fetched = []
    for request in range(request_total):
        resident_row = adapter_row_table[request_adapter[request]]
        owner = resident_row // resident_count
        store_position = resident_row % resident_count
        resident_down = lax.dynamic_index_in_dim(
            adapter_down_weight, store_position, 0, keepdims=False
        )
        resident_up = lax.dynamic_index_in_dim(adapter_up_weight, store_position, 0, keepdims=False)
        fetched.append(
            (broadcast(resident_down, "patch", owner), broadcast(resident_up, "patch", owner))
        )
    return fetched


def shards(
    hidden,
    skip,
    timestep_embedding_table,
    timesteps,
    group_norm_gain,
    group_norm_bias,
    kernel_weight,
    adapter_down_weight,
    adapter_up_weight,
    request_adapter,
    adapter_row_table,
):
    request_total, rows, width, chans = hidden.shape
    steps_count = timestep_embedding_table.shape[0]
    onehot = (timesteps[:, None] == jnp.arange(steps_count, dtype=jnp.int32)[None, :]).astype(
        jnp.float32
    )
    temb = jnp.dot(
        onehot,
        timestep_embedding_table,
        preferred_element_type=jnp.float32,
        precision=lax.Precision.HIGHEST,
    )
    shifted = hidden + temb[:, None, None, :]
    grouped = shifted.reshape(request_total, rows, width, GROUPS, chans // GROUPS)
    count = rows * lax.axis_size("patch") * width * (chans // GROUPS)
    totals = lax.psum(jnp.sum(grouped, axis=(1, 2, 4)), "patch")
    mean = totals / count
    centered = grouped - mean[:, None, None, :, None]
    squares = lax.psum(jnp.sum(centered * centered, axis=(1, 2, 4)), "patch")
    var = squares / count
    normed = (centered * lax.rsqrt(var + 1e-05)[:, None, None, :, None]).reshape(
        request_total, rows, width, chans
    )
    act = jax.nn.silu(normed * group_norm_gain + group_norm_bias).astype(jnp.bfloat16)
    extended = padded(act, (("patch", 1),), 1)
    extended = jnp.pad(extended, ((0, 0), (0, 0), (1, 1), (0, 0)))
    partner = from_partner(extended, "req", 0)
    taps = make_taps(jnp.concatenate([extended, partner], axis=0), rows, width)
    pixels = request_total * rows * width
    conv_half = jnp.einsum(
        "ptc,tco->po",
        taps,
        lax.all_gather(kernel_weight, "patch", axis=1, tiled=True),
        preferred_element_type=jnp.float32,
    )
    own_half = conv_half[:pixels]
    returned = from_partner(conv_half[pixels:], "req", 0)
    first = lax.axis_index("req") == 0
    left_half = jnp.where(first, own_half, returned)
    right_half = jnp.where(first, returned, own_half)
    conv = jnp.concatenate([left_half, right_half], axis=1).reshape(
        request_total, rows * width, chans
    )
    own_taps = taps[:pixels].reshape(request_total, rows * width, 9 * chans)
    adapter_factors = load_adapter_factors(
        adapter_down_weight, adapter_up_weight, request_adapter, adapter_row_table, request_total
    )
    deltas = []
    for request in range(request_total):
        down_factor, upper_limit = adapter_factors[request]
        low = lax.dot_general(
            own_taps[request],
            down_factor,
            (((1,), (1,)), ((), ())),
            preferred_element_type=jnp.float32,
        ).astype(jnp.bfloat16)
        deltas.append(jnp.dot(low, upper_limit, preferred_element_type=jnp.float32))
    total = conv + jnp.stack(deltas, axis=0)
    return skip + total.reshape(request_total, rows, width, chans)


def solution(mesh):
    def step(*args):
        n = lax.axis_size("patch")
        if fits(n, args[0], args[6], args[7]):
            return split_contraction(*args)
        return shards(*args)

    return jax.shard_map(
        step,
        mesh=mesh,
        in_specs=(
            P(("groups", "req"), "patch", None, None),
            P(("groups", "req"), "patch", None, None),
            P(),
            P(("groups", "req")),
            P(),
            P(),
            P(None, "patch", "req"),
            P(("groups", "patch"), None, None),
            P(("groups", "patch"), None, None),
            P(("groups", "req")),
            P("groups"),
        ),
        out_specs=P(("groups", "req"), "patch", None, None),
        check_vma=False,
    )
```

```python
import functools

import jax
import jax.numpy as jnp
from jax import lax
from jax.experimental import pallas as pl
from jax.experimental.pallas import tpu as pltpu
from jax.sharding import PartitionSpec as P

GROUPS = 32
LANES = 128
WIN = 256
MESH = pl.DeviceIdType.MESH
BF = jnp.bfloat16
F32 = jnp.float32


def hi_dot(a, b, dims):
    return lax.dot_general(
        a, b, (dims, ((), ())), precision=lax.Precision.HIGHEST, preferred_element_type=F32
    )


def block_kernel(
    n, own, reqs, width, chans,
    steps, asked, row_of, hid, skip, table, gain, bias, w_hbm, d_hbm, u_hbm,
    out,
    act, acts_in, taps, wpad, dfull, dpack, dall, uall, stat_out, stat_in,
    xsend, xrecv, keep, zsend, zrecv, lsend, lrecv,
    st_s, st_r, ac_s, ac_r, ac_l, d_s, d_r, d_l, w_s, w_r, w_l, dp_s, dp_r,
    x_s, x_r, z_s, z_r, l_s, l_r, u_s, u_f, u_r, u_l, up_s, up_r,
):
    me = lax.axis_index("patch")
    core = lax.axis_index("req")
    mate = 1 - core
    zs = n // 2
    z, x = me // 2, me % 2
    half = chans // 2
    rank = dall.shape[1]
    hrank = rank // 2
    per = d_hbm.shape[0]
    temb = [table[pl.ds(steps[r], 1), :] for r in range(reqs)]
    sel = [row_of[asked[r]] for r in range(reqs)]

    def window(j):
        return pl.multiple_of((j * own) // LANES * LANES, LANES)

    wpad[...] = jnp.zeros_like(wpad)

    barrier = pltpu.get_barrier_semaphore()
    for k in range(1, n):
        pl.semaphore_signal(barrier, inc=1, device_id={"patch": (me + k) % n}, device_id_type=MESH)
    pl.semaphore_signal(barrier, inc=1, device_id={"req": mate}, device_id_type=MESH)
    pl.semaphore_wait(barrier, n)

    inner = pl.multiple_of((me * own) % LANES, 32)

    def w_dst(t, c):
        return wpad.at[
            t // 3,
            pl.ds(pl.multiple_of((t % 3) * WIN + inner, 32), own),
            pl.ds(pl.multiple_of(c * half, LANES), half),
        ]

    def w_remote(t, c):
        return pltpu.make_async_remote_copy(
            src_ref=w_hbm.at[t], dst_ref=w_dst(t, c), send_sem=w_s.at[t], recv_sem=w_r.at[t],
            device_id={"req": mate}, device_id_type=MESH,
        )

    def w_local(t):
        return pltpu.make_async_copy(w_hbm.at[t], w_dst(t, core), w_l.at[t])

    for t in range(9):
        w_local(t).start()
        w_remote(t, core).start()

    rank_at = pl.multiple_of(core * hrank, hrank)

    def d_dst(src):
        return dall.at[pl.ds(src * per, per), pl.ds(rank_at, hrank), :]

    def d_copy(peer, src):
        return pltpu.make_async_remote_copy(
            src_ref=dpack.at[peer], dst_ref=d_dst(src),
            send_sem=d_s.at[peer], recv_sem=d_r.at[src],
            device_id={"patch": peer}, device_id_type=MESH,
        )

    d_load = pltpu.make_async_copy(d_hbm.at[:, pl.ds(rank_at, hrank), :], dfull, d_l)
    d_load.start()
    d_load.wait()
    for a in range(per):
        for j in range(n):
            parts = [dfull[a, :, t * chans + j * own : t * chans + (j + 1) * own] for t in range(9)]
            dpack[j, a] = jnp.concatenate(parts, axis=1)
    for k in range(1, n):
        d_copy((me + k) % n, me).start()
    d_dst(me)[...] = dpack[me]

    def u_dst(src):
        return uall.at[pl.ds(src * per, per), pl.ds(rank_at, hrank), :]

    near = me + 1 - 2 * x

    def u_copy(peer, src):
        return pltpu.make_async_remote_copy(
            src_ref=u_hbm.at[:, pl.ds(rank_at, hrank), :], dst_ref=u_dst(src),
            send_sem=u_s.at[peer], recv_sem=u_r.at[src],
            device_id={"patch": peer}, device_id_type=MESH,
        )

    def u_pass(src):
        return pltpu.make_async_remote_copy(
            src_ref=u_dst(src), dst_ref=u_dst(src), send_sem=u_f.at[src], recv_sem=u_r.at[src],
            device_id={"patch": near}, device_id_type=MESH,
        )

    u_own = pltpu.make_async_copy(u_hbm.at[:, pl.ds(rank_at, hrank), :], u_dst(me), u_l)

    def send_up():
        u_own.start()
        u_copy(near, me).start()
        for k in range(1, zs):
            u_copy((z + k) % zs * 2 + x, me).start()

    c_of = lax.broadcasted_iota(jnp.int32, (chans, LANES), 0)
    g_of = lax.broadcasted_iota(jnp.int32, (chans, LANES), 1)
    size = chans // GROUPS
    member = jnp.where((c_of >= g_of * size) & (c_of < (g_of + 1) * size), 1.0, 0.0).astype(F32)
    count = width * size
    sums = [
        jnp.sum(hid[r * width : (r + 1) * width, :] + temb[r], axis=0, keepdims=True)
        for r in range(reqs)
    ]
    pad = [jnp.zeros((8 - reqs, chans), F32)] if reqs < 8 else []
    mean = hi_dot(jnp.concatenate(sums + pad, axis=0), member, ((1,), (0,))) / count
    wide = hi_dot(mean, member, ((1,), (1,)))
    squares = []
    for r in range(reqs):
        c = hid[r * width : (r + 1) * width, :] + temb[r] - wide[r : r + 1, :]
        squares.append(jnp.sum(c * c, axis=0, keepdims=True))
    second = hi_dot(jnp.concatenate(squares + pad, axis=0), member, ((1,), (0,)))
    stat_out[0] = mean
    stat_out[1] = second

    def st_copy(peer, src):
        return pltpu.make_async_remote_copy(
            src_ref=stat_out, dst_ref=stat_in.at[src], send_sem=st_s.at[peer], recv_sem=st_r.at[src],
            device_id={"patch": peer}, device_id_type=MESH,
        )

    for k in range(1, n):
        st_copy((me + k) % n, me).start()
    stat_in[me] = stat_out[...]
    for k in range(1, n):
        st_copy((me + k) % n, (me + k) % n).wait_recv()
    means = stat_in[:, 0]
    total_mean = jnp.sum(means, axis=0) / n
    spread = means - total_mean[None]
    var = (jnp.sum(stat_in[:, 1], axis=0) + count * jnp.sum(spread * spread, axis=0)) / (count * n)
    mean_w = hi_dot(total_mean, member, ((1,), (1,)))
    inv_w = hi_dot(lax.rsqrt(var + 1e-05), member, ((1,), (1,)))
    for r in range(reqs):
        rows = slice(r * width, (r + 1) * width)
        v = (hid[rows, :] + temb[r] - mean_w[r : r + 1, :]) * inv_w[r : r + 1, :]
        v = v * gain[...] + bias[...]
        act[rows, :] = (v / (1.0 + jnp.exp(-v))).astype(BF)

    def ac_copy(peer, src):
        return pltpu.make_async_remote_copy(
            src_ref=act.at[:, pl.ds(window(peer), WIN)], dst_ref=acts_in.at[src],
            send_sem=ac_s.at[peer], recv_sem=ac_r.at[src],
            device_id={"patch": peer}, device_id_type=MESH,
        )

    ac_own = pltpu.make_async_copy(act.at[:, pl.ds(window(me), WIN)], acts_in.at[me], ac_l)
    for k in range(1, n):
        ac_copy((me + k) % n, me).start()
    ac_own.start()

    send_up()

    taps[0] = jnp.zeros(taps.shape[1:], BF)
    taps[n + 1] = jnp.zeros(taps.shape[1:], BF)
    cells = reqs * width
    px = lax.broadcasted_iota(jnp.int32, (cells, WIN), 0) % width
    ch = lax.broadcasted_iota(jnp.int32, (cells, WIN), 1)
    mine = (ch >= inner) & (ch < inner + own)

    def lay(y):
        v = jnp.where(mine, acts_in[y].astype(F32), 0.0)
        taps[y + 1, :, 0:WIN] = jnp.where(px == 0, 0.0, pltpu.roll(v, 1, 0)).astype(BF)
        taps[y + 1, :, WIN : 2 * WIN] = v.astype(BF)
        taps[y + 1, :, 2 * WIN :] = jnp.where(px == width - 1, 0.0, pltpu.roll(v, cells - 1, 0)).astype(BF)

    ac_own.wait()
    lay(me)

    @pl.loop(1, n)
    def _(k):
        y = (me + k) % n
        ac_copy(y, y).wait_recv()
        lay(y)

    for t in range(9):
        w_local(t).wait()
        w_remote(t, mate).wait_recv()

    def conv(y, put):
        @pl.loop(0, chans // WIN)
        def _(m):
            cols = pl.ds(pl.multiple_of(m * WIN, WIN), WIN)
            s = jnp.dot(taps[y], wpad[0, :, cols], preferred_element_type=F32)
            s += jnp.dot(taps[y + 1], wpad[1, :, cols], preferred_element_type=F32)
            s += jnp.dot(taps[y + 2], wpad[2, :, cols], preferred_element_type=F32)
            put(cols, s)

    def x_copy(i):
        return pltpu.make_async_remote_copy(
            src_ref=xsend.at[i], dst_ref=xrecv.at[i], send_sem=x_s.at[i], recv_sem=x_r.at[i],
            device_id={"patch": near}, device_id_type=MESH,
        )

    order = (3 * (1 - z // 2), (2 + 3 * z) % 5, 1 + z % 2, z)

    def z_copy(dest):
        up = dest > z
        after = jnp.where(up, z + 1, z - 1)
        slot = jnp.where(jnp.logical_and(dest < z, after == dest), zs, dest)
        return pltpu.make_async_remote_copy(
            src_ref=zsend.at[dest], dst_ref=zrecv.at[slot], send_sem=z_s.at[dest], recv_sem=z_r.at[slot],
            device_id={"patch": after * 2 + x}, device_id_type=MESH,
        )

    def z_arrival(slot):
        return pltpu.make_async_copy(zrecv.at[slot], zrecv.at[slot], z_r.at[slot])

    def forward(i):
        dest = order[i]
        x_copy(i).wait_recv()
        upward = jnp.logical_and(dest > z, z > 0)
        downward = jnp.logical_and(dest < z, z < zs - 1)

        @pl.when(jnp.logical_or(upward, downward))
        def _():
            z_arrival(dest).wait()
            keep[i] += zrecv[dest].astype(F32)

        zsend[dest] = (keep[i] + xrecv[i].astype(F32)).astype(BF)
        z_copy(dest).start()

    for i in range(zs):
        def put(cols, s, i=i):
            xsend[i, :, cols] = s.astype(BF)

        conv(order[i] * 2 + 1 - x, put)
        x_copy(i).start()

    for i in range(zs):
        def put(cols, s, i=i):
            keep[i, :, cols] = s

        conv(order[i] * 2 + x, put)

    for i in range(zs - 1):
        forward(i)

    for k in range(1, n):
        d_copy((me + k) % n, (me + k) % n).wait_recv()

    def dp_copy(at):
        part = dall.at[:, pl.ds(pl.multiple_of(at * hrank, hrank), hrank), :]
        return pltpu.make_async_remote_copy(
            src_ref=part, dst_ref=part, send_sem=dp_s, recv_sem=dp_r,
            device_id={"req": mate}, device_id_type=MESH,
        )

    dp_copy(core).start()
    for k in range(1, zs):
        src = (z + k) % zs * 2 + x
        u_copy(src, src).wait_recv()
        u_pass(src).start()
    dp_copy(mate).wait_recv()
    for q in range(reqs // 2):
        pair = []
        for r in (2 * q, 2 * q + 1):
            packed = dall[sel[r]].astype(F32)
            empty = jnp.zeros((rank, WIN - own), F32)
            spread_out = [
                pltpu.roll(jnp.concatenate([packed[:, t * own : (t + 1) * own], empty], axis=1), inner, 1)
                for t in range(9)
            ]
            factor = jnp.concatenate(spread_out, axis=1).astype(BF)
            low = jnp.zeros((n * width, rank), F32)
            for dy in range(3):
                lhs = taps[dy : dy + n, r * width : (r + 1) * width, :].reshape(n * width, 3 * WIN)
                low += lax.dot_general(
                    lhs, factor[:, dy * 3 * WIN : (dy + 1) * 3 * WIN], (((1,), (1,)), ((), ())),
                    preferred_element_type=F32,
                )
            pair.append(low)
        both = jnp.concatenate(pair, axis=1).astype(BF)
        lsend[:, q * width : (q + 1) * width, :] = both.reshape(n, width, 2 * rank)

    def l_copy(peer, src):
        return pltpu.make_async_remote_copy(
            src_ref=lsend.at[peer], dst_ref=lrecv.at[src], send_sem=l_s.at[peer], recv_sem=l_r.at[src],
            device_id={"patch": peer}, device_id_type=MESH,
        )

    for k in range(1, n):
        l_copy((me + k) % n, me).start()

    u_own.wait()
    u_copy(near, near).wait_recv()
    for k in range(1, zs):
        u_pass((z + k) % zs * 2 + 1 - x).wait_recv()

    def up_copy(at):
        part = uall.at[:, pl.ds(pl.multiple_of(at * hrank, hrank), hrank), :]
        return pltpu.make_async_remote_copy(
            src_ref=part, dst_ref=part, send_sem=up_s, recv_sem=up_r,
            device_id={"req": mate}, device_id_type=MESH,
        )

    up_copy(core).start()
    x_copy(zs - 1).wait_recv()
    out[...] = skip[...] + keep[zs - 1] + xrecv[zs - 1].astype(F32)

    @pl.when(z > 0)
    def _():
        z_arrival(z).wait()
        out[...] += zrecv[z].astype(F32)

    @pl.when(z < zs - 1)
    def _():
        z_arrival(zs).wait()
        out[...] += zrecv[zs].astype(F32)

    up_copy(mate).wait_recv()
    both = lsend[me].astype(F32)
    for k in range(1, n):
        src = (me + k) % n
        l_copy(src, src).wait_recv()
        both += lrecv[src].astype(F32)
    both = both.astype(BF)
    for r in range(reqs):
        low = both[r // 2 * width : (r // 2 + 1) * width, r % 2 * rank : (r % 2 + 1) * rank]
        out[r * width : (r + 1) * width, :] += jnp.dot(low, uall[sel[r]], preferred_element_type=F32)

    dp_copy(core).wait_send()
    up_copy(core).wait_send()
    u_copy(near, me).wait_send()
    for k in range(1, zs):
        u_copy((z + k) % zs * 2 + x, me).wait_send()
        u_pass((z + k) % zs * 2 + x).wait_send()
    for t in range(9):
        w_remote(t, core).wait_send()
    for k in range(1, n):
        st_copy((me + k) % n, me).wait_send()
        ac_copy((me + k) % n, me).wait_send()
        l_copy((me + k) % n, me).wait_send()

    for k in range(1, n):
        d_copy((me + k) % n, me).wait_send()

    @pl.loop(0, zs)
    def _(i):
        x_copy(i).wait_send()

    for i in range(zs - 1):
        z_copy(order[i]).wait_send()


def run_block(n, steps, asked, row_of, hid, skip, table, gain, bias, weight, down, up):
    cells, chans = hid.shape
    reqs = asked.shape[0]
    width = cells // reqs
    own = weight.shape[1]
    per, rank, _ = down.shape
    zs = n // 2
    dma = pltpu.SemaphoreType.DMA
    vmem = pl.BlockSpec(memory_space=pltpu.VMEM)
    hbm = pl.BlockSpec(memory_space=pl.ANY)
    smem = pl.BlockSpec(memory_space=pltpu.SMEM)
    return pl.pallas_call(
        functools.partial(block_kernel, n, own, reqs, width, chans),
        out_shape=jax.ShapeDtypeStruct((cells, chans), F32),
        in_specs=[smem] * 3 + [vmem] * 5 + [hbm] * 3,
        out_specs=vmem,
        scratch_shapes=[
            pltpu.VMEM((cells, chans), BF),
            pltpu.VMEM((n, cells, WIN), BF),
            pltpu.VMEM((n + 2, cells, 3 * WIN), BF),
            pltpu.VMEM((3, 3 * WIN, chans), BF),
            pltpu.VMEM((per, rank // 2, 9 * chans), BF),
            pltpu.VMEM((n, per, rank // 2, 9 * own), BF),
            pltpu.VMEM((n * per, rank, 9 * own), BF),
            pltpu.VMEM((n * per, rank, chans), BF),
            pltpu.VMEM((2, 8, LANES), F32),
            pltpu.VMEM((n, 2, 8, LANES), F32),
            pltpu.VMEM((zs, cells, chans), BF),
            pltpu.VMEM((zs, cells, chans), BF),
            pltpu.VMEM((zs, cells, chans), F32),
            pltpu.VMEM((zs, cells, chans), BF),
            pltpu.VMEM((zs + 1, cells, chans), BF),
            pltpu.VMEM((n, cells // 2, 2 * rank), BF),
            pltpu.VMEM((n, cells // 2, 2 * rank), BF),
            dma((n,)), dma((n,)),
            dma((n,)), dma((n,)), dma,
            dma((n,)), dma((n,)), dma,
            dma((9,)), dma((9,)), dma((9,)),
            dma, dma,
            dma((zs,)), dma((zs,)),
            dma((zs,)), dma((zs + 1,)),
            dma((n,)), dma((n,)),
            dma((n,)), dma((n,)), dma((n,)), dma,
            dma, dma,
        ],
        compiler_params=pltpu.CompilerParams(
            collective_id=0, has_side_effects=True, vmem_limit_bytes=56 * 2**20
        ),
        cost_estimate=pl.CostEstimate(
            flops=2 * n * cells * 9 * WIN * chans, bytes_accessed=10**8, transcendentals=0
        ),
    )(steps, asked, row_of, hid, skip, table, gain, bias, weight, down, up)


def split_contraction(
    hidden, skip, timestep_embedding_table, timesteps, group_norm_gain, group_norm_bias,
    kernel_weight, adapter_down_weight, adapter_up_weight, request_adapter, adapter_row_table,
):
    shape = hidden.shape
    flat = (shape[0] * shape[1] * shape[2], shape[3])
    return run_block(
        lax.axis_size("patch"), timesteps, request_adapter, adapter_row_table,
        hidden.reshape(flat), skip.reshape(flat), timestep_embedding_table,
        group_norm_gain[None], group_norm_bias[None],
        kernel_weight, adapter_down_weight, adapter_up_weight,
    ).reshape(shape)


def fits(n, hidden, kernel_weight, down):
    own = kernel_weight.shape[1]
    ends = all(j * own // LANES * LANES + WIN <= hidden.shape[3] and j * own % LANES + own <= WIN for j in range(n))
    return (
        n == 8 and hidden.shape[1] == 1 and hidden.shape[0] in (2, 4, 6, 8)
        and own % 32 == 0 and ends and down.shape[1] == 64
    )


def broadcast(block, axis, owner):
    block = jnp.where(lax.axis_index(axis) == owner, block, jnp.zeros_like(block))
    return lax.psum(block, axis)


def padded(cells, sides, width):
    for axis, dim in sides:
        count = lax.axis_size(axis)
        ends = count - 1
        head = lax.slice_in_dim(cells, 0, width, axis=dim)
        tail = lax.slice_in_dim(cells, cells.shape[dim] - width, cells.shape[dim], axis=dim)
        cells = jnp.concatenate(
            [
                lax.ppermute(tail, axis, [(i, (i + 1) % count) for i in range(ends)]),
                cells,
                lax.ppermute(head, axis, [((i + 1) % count, i) for i in range(ends)]),
            ],
            axis=dim,
        )
    return cells


def from_partner(x, axis, stride):
    return lax.ppermute(x, axis, [(i, i ^ 1 << stride) for i in range(lax.axis_size(axis))])


def make_taps(extended, rows, width):
    pieces = [extended[:, dy : dy + rows, dx : dx + width, :] for dy in range(3) for dx in range(3)]
    stacked = jnp.stack(pieces, axis=3)
    count = stacked.shape[0] * rows * width
    return stacked.reshape(count, 9, stacked.shape[-1])


def load_adapter_factors(
    adapter_down_weight, adapter_up_weight, request_adapter, adapter_row_table, request_total
):
    resident_count = adapter_down_weight.shape[0]
    fetched = []
    for request in range(request_total):
        resident_row = adapter_row_table[request_adapter[request]]
        owner = resident_row // resident_count
        store_position = resident_row % resident_count
        resident_down = lax.dynamic_index_in_dim(
            adapter_down_weight, store_position, 0, keepdims=False
        )
        resident_up = lax.dynamic_index_in_dim(adapter_up_weight, store_position, 0, keepdims=False)
        fetched.append(
            (broadcast(resident_down, "patch", owner), broadcast(resident_up, "patch", owner))
        )
    return fetched


def shards(
    hidden,
    skip,
    timestep_embedding_table,
    timesteps,
    group_norm_gain,
    group_norm_bias,
    kernel_weight,
    adapter_down_weight,
    adapter_up_weight,
    request_adapter,
    adapter_row_table,
):
    request_total, rows, width, chans = hidden.shape
    steps_count = timestep_embedding_table.shape[0]
    onehot = (timesteps[:, None] == jnp.arange(steps_count, dtype=jnp.int32)[None, :]).astype(
        jnp.float32
    )
    temb = jnp.dot(
        onehot,
        timestep_embedding_table,
        preferred_element_type=jnp.float32,
        precision=lax.Precision.HIGHEST,
    )
    shifted = hidden + temb[:, None, None, :]
    grouped = shifted.reshape(request_total, rows, width, GROUPS, chans // GROUPS)
    count = rows * lax.axis_size("patch") * width * (chans // GROUPS)
    totals = lax.psum(jnp.sum(grouped, axis=(1, 2, 4)), "patch")
    mean = totals / count
    centered = grouped - mean[:, None, None, :, None]
    squares = lax.psum(jnp.sum(centered * centered, axis=(1, 2, 4)), "patch")
    var = squares / count
    normed = (centered * lax.rsqrt(var + 1e-05)[:, None, None, :, None]).reshape(
        request_total, rows, width, chans
    )
    act = jax.nn.silu(normed * group_norm_gain + group_norm_bias).astype(jnp.bfloat16)
    extended = padded(act, (("patch", 1),), 1)
    extended = jnp.pad(extended, ((0, 0), (0, 0), (1, 1), (0, 0)))
    partner = from_partner(extended, "req", 0)
    taps = make_taps(jnp.concatenate([extended, partner], axis=0), rows, width)
    pixels = request_total * rows * width
    conv_half = jnp.einsum(
        "ptc,tco->po",
        taps,
        lax.all_gather(kernel_weight, "patch", axis=1, tiled=True),
        preferred_element_type=jnp.float32,
    )
    own_half = conv_half[:pixels]
    returned = from_partner(conv_half[pixels:], "req", 0)
    first = lax.axis_index("req") == 0
    left_half = jnp.where(first, own_half, returned)
    right_half = jnp.where(first, returned, own_half)
    conv = jnp.concatenate([left_half, right_half], axis=1).reshape(
        request_total, rows * width, chans
    )
    own_taps = taps[:pixels].reshape(request_total, rows * width, 9 * chans)
    adapter_factors = load_adapter_factors(
        adapter_down_weight, adapter_up_weight, request_adapter, adapter_row_table, request_total
    )
    deltas = []
    for request in range(request_total):
        down_factor, upper_limit = adapter_factors[request]
        low = lax.dot_general(
            own_taps[request],
            down_factor,
            (((1,), (1,)), ((), ())),
            preferred_element_type=jnp.float32,
        ).astype(jnp.bfloat16)
        deltas.append(jnp.dot(low, upper_limit, preferred_element_type=jnp.float32))
    total = conv + jnp.stack(deltas, axis=0)
    return skip + total.reshape(request_total, rows, width, chans)


def solution(mesh):
    def step(*args):
        n = lax.axis_size("patch")
        if fits(n, args[0], args[6], args[7]):
            return split_contraction(*args)
        return shards(*args)

    return jax.shard_map(
        step,
        mesh=mesh,
        in_specs=(
            P(("groups", "req"), "patch", None, None),
            P(("groups", "req"), "patch", None, None),
            P(),
            P(("groups", "req")),
            P(),
            P(),
            P(None, "patch", "req"),
            P(("groups", "patch"), None, None),
            P(("groups", "patch"), None, None),
            P(("groups", "req")),
            P("groups"),
        ),
        out_specs=P(("groups", "req"), "patch", None, None),
        check_vma=False,
    )
```
